256 devices in a mesh: doc: 64 (over x, z, core), feat: 4 (over y).
Axes of the slice: x: 4, y: 4, z: 8, core: 2. Of those that a mesh axis runs over, the one named last changes fastest.
Arguments:
- b_tiles: bfloat16 [12288, 512, 128], P('doc', 'feat'), may hold values from -0.0625 to 0.0625
- b_rows: int32 [12288, 4], P('doc', 'feat'), may hold values from 0 to 11, as said below
- b_cols: int32 [12288, 4], P('doc', 'feat'), may hold values from 0 to 4095
- b_count: int32 [64, 4], P('doc', 'feat'), may hold values from 144 to 192
- b_offsets: int32 [65], replicated, may hold values from 0 to 480, as said below
- a_tiles: bfloat16 [4096, 512, 128], P('doc', 'feat'), may hold values from -0.375 to 0.375
- a_rows: int32 [4096, 4], P('doc', 'feat'), may hold values from 0 to 12, as said below
- a_tags: int32 [4096, 4], P('doc', 'feat'), may hold values from 0 to 8191, as said below
- a_count: int32 [64, 4], P('doc', 'feat'), may hold values from 48 to 64
- a_offsets: int32 [65], replicated, may hold values from 0 to 480, as said below
- omega_seed: int32 [1], replicated, may hold values from 0 to 1073741823
Outputs:
- tag_sketch: float32 [1048576, 256], P(('doc', 'feat'))
The draws below stay inside these ranges and needn't reach their ends.
Inputs may be any that keep to these rules, and one draw needn't show every extreme that they name: b_offsets[0] is 0 and each device's range of the text view holds 3 to 12 row blocks. a_offsets[0] is 0 and a_offsets[64] equals b_offsets[64]; every other entry lies 1 to 2 row blocks below the same entry of b_offsets; each device's range of the tag view holds at most 13 row blocks. `b_rows`: below the number of row blocks of the device's range of the text view. `a_rows`: below the number of row blocks of the device's range of the tag view. `a_tags`: the rows of a tile's tag block lie, under the output's placement, on a device with the same feat index as the tile; on one device at most 2 tiles in use have tag blocks on devices of one doc index, and in every draw some doc index gets exactly 2 tiles in use from every device.
All inputs are finite; a program needn't handle non-finite values.
Results may differ from the reference program's by a relative error of at most 0.004.
Values may be sent and summed in bfloat16 or wider, within the bound.
A program may use at most 128 MiB of HBM per device.

```python
import jax
import jax.numpy as jnp
from jax import lax

TILE = 128
SKETCH = 256
TERMS = 2097152
TAG_DEV = 4096
TILES_B = 192
TILES_A = 64
ROWB_MAX = 12
MARGIN = 2
CAPT = 2
TAGS = 1048576
N_DOC = 64
N_FEAT = 4


def split_draw(key):
    k_len, k_gap, k_pick = jax.random.split(jax.random.fold_in(key, 7001), 3)
    half_len = jax.random.randint(k_len, (N_DOC // 2,), MARGIN + 1, ROWB_MAX + 1).astype(jnp.int32)
    b_len = jnp.stack([half_len, MARGIN + 1 + ROWB_MAX - half_len], axis=1).reshape(N_DOC).astype(jnp.int32)
    boundary_gap = jax.random.randint(k_gap, (N_DOC + 1,), 1, MARGIN + 1).astype(jnp.int32)
    boundary_gap = boundary_gap.at[N_DOC - 1].set(jnp.minimum(boundary_gap[N_DOC - 1], MARGIN - 1))
    widest = jax.random.randint(k_pick, (), 1, N_DOC - 1).astype(jnp.int32)
    partner = jnp.bitwise_xor(widest, 1)
    b_len = b_len.at[widest].set(ROWB_MAX).at[partner].set(MARGIN + 1)
    boundary_gap = boundary_gap.at[widest].set(MARGIN).at[widest + 1].set(1)
    boundary_gap = boundary_gap.at[0].set(0).at[N_DOC].set(0)
    b_off = jnp.concatenate([jnp.zeros((1,), jnp.int32), jnp.cumsum(b_len).astype(jnp.int32)])
    a_off = (b_off - boundary_gap).astype(jnp.int32)
    return (b_off, a_off)


def local_rows(key, offsets, tiles, salt):
    lengths = offsets[1:] - offsets[:-1]
    raw_bits = jax.random.randint(jax.random.fold_in(key, salt), (N_DOC, tiles, N_FEAT), 0, 1048576).astype(jnp.int32)
    rows = raw_bits % lengths[:, None, None]
    rows = rows.at[:, 0, :].set(jnp.broadcast_to(lengths[:, None] - 1, (N_DOC, N_FEAT)))
    rows = rows.at[:, 1, :].set(0)
    return rows.reshape(N_DOC * tiles, N_FEAT).astype(jnp.int32)


def tile_counts(key, tiles, salt):
    k_count, k_spot = jax.random.split(jax.random.fold_in(key, salt), 2)
    counts = jax.random.randint(k_count, (N_DOC * N_FEAT,), tiles * 3 // 4, tiles + 1).astype(jnp.int32)
    spot = jax.random.randint(k_spot, (), 0, N_DOC * N_FEAT)
    return counts.at[spot].set(tiles).reshape(N_DOC, N_FEAT)


def draw_b_offsets(key, part):
    return split_draw(key)[0]


def draw_a_offsets(key, part):
    return split_draw(key)[1]


def draw_b_rows(key, part):
    return local_rows(key, split_draw(key)[0], TILES_B, 7002)


def draw_a_rows(key, part):
    return local_rows(key, split_draw(key)[1], TILES_A, 7003)


def draw_b_count(key, part):
    return tile_counts(key, TILES_B, 7004)


def draw_a_count(key, part):
    return tile_counts(key, TILES_A, 7005)


def draw_a_tags(key, part):
    k_full, k_perm, k_low, k_high, k_blk = jax.random.split(jax.random.fold_in(key, 7006), 5)
    devices_all = N_DOC * N_FEAT
    full_owner = jax.random.randint(k_full, (), 0, N_DOC).astype(jnp.int32)
    spread_len = (N_DOC - 1) * CAPT
    position = jnp.arange(spread_len, dtype=jnp.int32)
    spread = position // CAPT
    spread = spread + (spread >= full_owner).astype(jnp.int32)
    first_copy = (position % CAPT == 0) & ((spread == 0) | (spread == N_DOC - 1))
    priority = jnp.where(first_copy, 0, 1).astype(jnp.int32)

    def order_one(one_key):
        ranks = jax.random.permutation(one_key, spread_len).astype(jnp.int32)
        scores = priority * spread_len + ranks
        return spread[jnp.argsort(scores, stable=True)]
    others = jax.vmap(order_one)(jax.random.split(k_perm, devices_all))
    others = others[:, :TILES_A - CAPT].astype(jnp.int32)
    owners = jnp.concatenate([jnp.full((devices_all, CAPT), 1, jnp.int32) * full_owner, others], axis=1)
    owned_blocks = TAG_DEV // TILE
    inner = jax.random.randint(k_blk, (devices_all, TILES_A), 0, owned_blocks).astype(jnp.int32)
    slot_iota = jnp.arange(TILES_A, dtype=jnp.int32)[None, :]
    first_low = jnp.argmax(owners == 0, axis=1).astype(jnp.int32)[:, None]
    first_high = jnp.argmax(owners == N_DOC - 1, axis=1).astype(jnp.int32)[:, None]
    inner = jnp.where(slot_iota == first_low, 0, inner)
    inner = jnp.where(slot_iota == first_high, owned_blocks - 1, inner).astype(jnp.int32)
    half_tiles = TILES_A // 2
    low_order = jax.vmap(lambda k: jax.random.permutation(k, half_tiles))(jax.random.split(k_low, devices_all)).astype(jnp.int32)
    high_order = jax.vmap(lambda k: jax.random.permutation(k, TILES_A - half_tiles))(jax.random.split(k_high, devices_all)).astype(jnp.int32)
    owners = jnp.concatenate([jnp.take_along_axis(owners[:, :half_tiles], low_order, axis=1), jnp.take_along_axis(owners[:, half_tiles:], high_order, axis=1)], axis=1)
    inner = jnp.concatenate([jnp.take_along_axis(inner[:, :half_tiles], low_order, axis=1), jnp.take_along_axis(inner[:, half_tiles:], high_order, axis=1)], axis=1)
    feat_of = (jnp.arange(devices_all, dtype=jnp.int32) % N_FEAT)[:, None]
    tags = (owners * N_FEAT + feat_of) * owned_blocks + inner
    return tags.reshape(N_DOC, N_FEAT, TILES_A).transpose(0, 2, 1).reshape(N_DOC * TILES_A, N_FEAT).astype(jnp.int32)


def plant(values, stream_key, least, high):
    longest = values.shape.index(max(values.shape))
    spots = []
    for shift in (0, 1):
        where = [jax.random.randint(jax.random.fold_in(stream_key, axis), (), 0, length) for axis, length in enumerate(values.shape)]
        where[longest] = (where[longest] + shift) % values.shape[longest]
        spots.append(tuple(where))
    return values.at[spots[0]].set(least).at[spots[1]].set(high)


def level_of(key, extent, shards, least, top_value):
    factor_of = 1.0
    for axis_at, parts in shards:
        draws = jax.random.uniform(jax.random.fold_in(jax.random.fold_in(key, 6), axis_at), (parts,), jnp.float32, least / len(shards), top_value / len(shards))
        factor_of = factor_of * jnp.repeat(jnp.exp(draws), extent[axis_at] // parts).reshape((-1,) + (1,) * (len(extent) - 1 - axis_at))
    return factor_of


def scatter_about(key, shape, deviation, bound, pieces=(), held_as=jnp.bfloat16):
    result = deviation * jax.random.normal(key, shape, jnp.float32)
    if pieces:
        result = result * level_of(key, shape, pieces, -0.22, 0.18)
    return jnp.clip(result, -bound, bound).astype(held_as)


def setup_inputs(seed: int = 0) -> dict:
    arg_keys = jax.random.split(jax.random.key(seed), 12)
    return {
        "b_tiles": scatter_about(arg_keys[0], (N_DOC * TILES_B, N_FEAT * TILE, TILE), (N_FEAT * TILE * TILES_B // ROWB_MAX) ** -0.5, 0.0625, ((0, 64), (1, 4))),
        "b_rows": draw_b_rows(jax.random.fold_in(arg_keys[11], 71), 0),
        "b_cols": plant(jax.random.randint(arg_keys[2], (N_DOC * TILES_B, N_FEAT), 0, TERMS // (TILE * N_FEAT)), jax.random.fold_in(arg_keys[2], 1), 0, (TERMS // (TILE * N_FEAT)) - 1).astype(jnp.int32),
        "b_count": draw_b_count(jax.random.fold_in(arg_keys[11], 71), 0),
        "b_offsets": draw_b_offsets(jax.random.fold_in(arg_keys[11], 71), 0),
        "a_tiles": scatter_about(arg_keys[5], (N_DOC * TILES_A, N_FEAT * TILE, TILE), (2 * TILE) ** -0.5, 0.375, ((0, 64), (1, 4))),
        "a_rows": draw_a_rows(jax.random.fold_in(arg_keys[11], 71), 0),
        "a_tags": draw_a_tags(jax.random.fold_in(arg_keys[11], 71), 0),
        "a_count": draw_a_count(jax.random.fold_in(arg_keys[11], 71), 0),
        "a_offsets": draw_a_offsets(jax.random.fold_in(arg_keys[11], 71), 0),
        "omega_seed": jax.random.randint(arg_keys[10], (1,), 0, 1073741824).astype(jnp.int32),
    }


def unsigned_shift(value, count):
    return lax.shift_right_logical(value, jnp.full(value.shape, count, jnp.int32))


def omega_panel(term_blocks, seed_value):
    row_iota = lax.broadcasted_iota(jnp.int32, (1, TILE, SKETCH), 1)
    col_iota = lax.broadcasted_iota(jnp.int32, (1, TILE, SKETCH), 2)
    mixing = (term_blocks.astype(jnp.int32)[:, None, None] * TILE + row_iota) * SKETCH + col_iota
    mixing = mixing ^ (seed_value.astype(jnp.int32) * 747796405)
    mixing = mixing ^ unsigned_shift(mixing, 16)
    mixing = mixing * 2146121005
    mixing = mixing ^ unsigned_shift(mixing, 15)
    mixing = mixing * (-2073254261)
    mixing = mixing ^ unsigned_shift(mixing, 16)
    levels = (unsigned_shift(mixing, 8) & 65535).astype(jnp.float32)
    return ((levels - 32767.5) * (3.4641016 / 65536.0)).astype(jnp.bfloat16)


def reference(b_tiles, b_rows, b_cols, b_count, b_offsets, a_tiles, a_rows, a_tags, a_count, a_offsets, omega_seed):
    seed_value = omega_seed[0]
    slab_blocks = TERMS // (TILE * N_FEAT)
    tile_ids_b = jnp.arange(TILES_B, dtype=jnp.int32)
    tile_ids_a = jnp.arange(TILES_A, dtype=jnp.int32)
    highest = lax.Precision.HIGHEST

    def add_text(running, doc_index):
        start = (doc_index * TILES_B).astype(jnp.int32)
        for feat_index in range(N_FEAT):
            tile_block = lax.dynamic_slice(b_tiles, (start, jnp.int32(feat_index * TILE), jnp.int32(0)), (TILES_B, TILE, TILE))
            row_local = lax.dynamic_slice(b_rows, (start, jnp.int32(feat_index)), (TILES_B, 1))[:, 0]
            col_local = lax.dynamic_slice(b_cols, (start, jnp.int32(feat_index)), (TILES_B, 1))[:, 0]
            panels = omega_panel(col_local + feat_index * slab_blocks, seed_value)
            products = jnp.einsum("tij,tjk->tik", tile_block.astype(jnp.float32), panels.astype(jnp.float32), precision=highest)
            live_mask = (tile_ids_b < b_count[doc_index, feat_index]).astype(jnp.float32)
            running = running.at[b_offsets[doc_index] + row_local].add(products * live_mask[:, None, None])
        return running, None

    z_accum, _ = lax.scan(add_text, jnp.zeros((N_DOC * ROWB_MAX, TILE, SKETCH), jnp.float32), jnp.arange(N_DOC, dtype=jnp.int32))
    z_doc = z_accum.astype(jnp.bfloat16)

    def add_tags(running, doc_index):
        start = (doc_index * TILES_A).astype(jnp.int32)
        for feat_index in range(N_FEAT):
            tile_block = lax.dynamic_slice(a_tiles, (start, jnp.int32(feat_index * TILE), jnp.int32(0)), (TILES_A, TILE, TILE))
            row_local = lax.dynamic_slice(a_rows, (start, jnp.int32(feat_index)), (TILES_A, 1))[:, 0]
            tag_local = lax.dynamic_slice(a_tags, (start, jnp.int32(feat_index)), (TILES_A, 1))[:, 0]
            sketch_rows = jnp.take(z_doc, a_offsets[doc_index] + row_local, axis=0).astype(jnp.float32)
            products = jnp.einsum("tij,tik->tjk", tile_block.astype(jnp.float32), sketch_rows, precision=highest)
            live_mask = (tile_ids_a < a_count[doc_index, feat_index]).astype(jnp.float32)
            running = running.at[tag_local].add(products * live_mask[:, None, None])
        return running, None

    y_accum, _ = lax.scan(add_tags, jnp.zeros((TAGS // TILE, TILE, SKETCH), jnp.float32), jnp.arange(N_DOC, dtype=jnp.int32))
    return y_accum.reshape(TAGS, SKETCH)
```

```python
import functools

import jax
import jax.numpy as jnp
from jax import lax
from jax.experimental import pallas as pl
from jax.experimental.pallas import tpu as pltpu
from jax.sharding import PartitionSpec as P

TILE = 128
SKETCH = 256
TERMS = 2097152
TAG_DEV = 4096
ROWB_MAX = 12
OWNED = TAG_DEV // TILE
N_DOC = 64
N_FEAT = 4
META = 16
PAGE = 2 * TILE + META
CHUNK = 16
GROUP = 4
DEPTH = 8

VMEM = pltpu.MemorySpace.VMEM
SMEM = pltpu.MemorySpace.SMEM
ANY = pl.ANY


def shr(value, count):
    return lax.shift_right_logical(value, jnp.full(value.shape, count, jnp.int32))


def text_kernel(rows, cols, count, seed, tiles, out, acc, base):
    step = pl.program_id(0)

    @pl.when(step == 0)
    def _():
        row_iota = lax.broadcasted_iota(jnp.int32, (TILE, SKETCH), 0)
        col_iota = lax.broadcasted_iota(jnp.int32, (TILE, SKETCH), 1)
        start = (row_iota * SKETCH + col_iota) ^ (seed[0] * 747796405)
        base[...] = start ^ shr(start, 16)
        acc[...] = jnp.zeros_like(acc)

    slab = lax.axis_index("feat") * (TERMS // (TILE * N_FEAT))
    used = count[0]

    def some(group, carry):
        products = []
        for lane in range(GROUP):
            at = group * GROUP + lane
            block = (cols[step * CHUNK + at] + slab) * (TILE * SKETCH)
            block = block ^ lax.shift_right_logical(block, jnp.int32(16))
            mixing = base[...] ^ block
            mixing = mixing * 2146121005
            mixing = mixing ^ shr(mixing, 15)
            mixing = mixing * -2073254261
            mixing = mixing ^ shr(mixing, 16)
            levels = (shr(mixing, 8) & 65535).astype(jnp.float32)
            panel = ((levels - 32767.5) * (3.4641016 / 65536.0)).astype(jnp.bfloat16)
            products.append(jnp.dot(tiles[at], panel, preferred_element_type=jnp.float32))
        for lane in range(GROUP):
            at = step * CHUNK + group * GROUP + lane
            place = jnp.where(at < used, rows[at], ROWB_MAX)
            acc[place] += products[lane]
        return carry

    left = jnp.clip(used - step * CHUNK, 0, CHUNK)
    lax.fori_loop(0, (left + GROUP - 1) // GROUP, some, 0)

    @pl.when(step == pl.num_programs(0) - 1)
    def _():
        out[...] = acc[0:ROWB_MAX]


def text_stage(b_rows, b_cols, b_count, omega_seed, b_tiles):
    tiles_b = b_tiles.shape[0]
    return pl.pallas_call(
        text_kernel,
        out_shape=jax.ShapeDtypeStruct((ROWB_MAX, TILE, SKETCH), jnp.float32),
        grid=(tiles_b // CHUNK,),
        in_specs=[
            pl.BlockSpec(memory_space=SMEM),
            pl.BlockSpec(memory_space=SMEM),
            pl.BlockSpec(memory_space=SMEM),
            pl.BlockSpec(memory_space=SMEM),
            pl.BlockSpec((CHUNK, TILE, TILE), lambda i: (i, 0, 0)),
        ],
        out_specs=pl.BlockSpec((ROWB_MAX, TILE, SKETCH), lambda i: (0, 0, 0)),
        scratch_shapes=[
            pltpu.VMEM((ROWB_MAX + 1, TILE, SKETCH), jnp.float32),
            pltpu.VMEM((TILE, SKETCH), jnp.int32),
        ],
        cost_estimate=pl.CostEstimate(flops=1700000000, bytes_accessed=8000000, transcendentals=0),
    )(b_rows, b_cols, b_count, omega_seed, b_tiles)


def pack_kernel(tags, rows, count, tiles, outbox, meta, seen, notes, sems, meta_sem):
    used = count[0]

    def clear(owner, carry):
        seen[owner] = 0
        for lane in range(4):
            notes[owner * 4 + lane] = 0
        return carry

    lax.fori_loop(0, N_DOC, clear, 0)

    def copy(at, owner, rank):
        start = pl.multiple_of(rank * TILE, TILE)
        return pltpu.make_async_copy(
            tiles.at[at], outbox.at[owner, pl.ds(start, TILE), :], sems.at[at]
        )

    def send(at, carry):
        tag = tags[at]
        owner = lax.shift_right_logical(tag, jnp.int32(7))
        rank = jnp.minimum(seen[owner], 1)
        seen[owner] = rank + 1
        notes[owner * 4 + rank * 2] = (tag & (OWNED - 1)) + 1
        notes[owner * 4 + rank * 2 + 1] = rows[at]
        copy(at, owner, rank).start()
        return carry

    lax.fori_loop(0, used, send, 0)
    lane_iota = lax.broadcasted_iota(jnp.int32, (META, TILE), 1)

    def note(owner, carry):
        value = jnp.zeros((META, TILE), jnp.int32)
        for lane in range(4):
            value = jnp.where(lane_iota == lane, notes[owner * 4 + lane], value)
        meta[owner] = value.astype(jnp.float32).astype(jnp.bfloat16)
        return carry

    lax.fori_loop(0, N_DOC, note, 0)
    last = pltpu.make_async_copy(meta, outbox.at[:, pl.ds(2 * TILE, META), :], meta_sem)
    last.start()

    def drain(at, carry):
        copy(at, 0, 0).wait()
        return carry

    lax.fori_loop(0, used, drain, 0)
    last.wait()


def pack_stage(a_tags, a_rows, a_count, a_tiles):
    tiles_a = a_tiles.shape[0]
    return pl.pallas_call(
        pack_kernel,
        out_shape=jax.ShapeDtypeStruct((N_DOC, PAGE, TILE), jnp.bfloat16),
        in_specs=[
            pl.BlockSpec(memory_space=SMEM),
            pl.BlockSpec(memory_space=SMEM),
            pl.BlockSpec(memory_space=SMEM),
            pl.BlockSpec(memory_space=VMEM),
        ],
        out_specs=pl.BlockSpec(memory_space=ANY),
        scratch_shapes=[
            pltpu.VMEM((N_DOC, META, TILE), jnp.bfloat16),
            pltpu.SMEM((N_DOC,), jnp.int32),
            pltpu.SMEM((N_DOC * 4,), jnp.int32),
            pltpu.SemaphoreType.DMA((tiles_a,)),
            pltpu.SemaphoreType.DMA,
        ],
    )(a_tags, a_rows, a_count, a_tiles)


def final_kernel(notes, b_offsets, a_offsets, inbox, gathered, out, lists, zbuf, sems):
    def listed(doc, found):
        shift = a_offsets[doc] - b_offsets[doc]
        before = b_offsets[doc] - b_offsets[jnp.maximum(doc - 1, 0)]
        for rank in range(2):
            tag = notes[doc * 4 + rank * 2] - 1
            row = notes[doc * 4 + rank * 2 + 1] + shift
            index = jnp.where(
                row < 0, (doc - 1) * ROWB_MAX + row + before, doc * ROWB_MAX + row
            )
            lists[0, found] = tag
            lists[1, found] = jnp.maximum(index, 0)
            lists[2, found] = doc * 2 + rank
            found = found + (tag >= 0).astype(jnp.int32)
        return found

    total = lax.fori_loop(0, N_DOC, listed, 0)

    def fetch(at, slot):
        return pltpu.make_async_copy(gathered.at[lists[1, at]], zbuf.at[slot], sems.at[slot])

    for first in range(DEPTH):

        @pl.when(first < total)
        def _():
            fetch(first, first).start()

    out[...] = jnp.zeros_like(out)

    def add(at, carry):
        slot = lax.rem(at, DEPTH)
        fetch(at, slot).wait()
        source = lists[2, at]
        start = pl.multiple_of((source & 1) * TILE, TILE)
        tile = inbox[lax.shift_right_logical(source, jnp.int32(1)), pl.ds(start, TILE), :]
        product = lax.dot_general(
            tile, zbuf[slot], (((0,), (0,)), ((), ())), preferred_element_type=jnp.float32
        )
        place = pl.multiple_of(lists[0, at] * TILE, TILE)
        out[pl.ds(place, TILE), :] += product

        @pl.when(at + DEPTH < total)
        def _():
            fetch(at + DEPTH, slot).start()

        return carry

    lax.fori_loop(0, total, add, 0)


def final_stage(notes, b_offsets, a_offsets, inbox, gathered):
    return pl.pallas_call(
        final_kernel,
        out_shape=jax.ShapeDtypeStruct((TAG_DEV, SKETCH), jnp.float32),
        in_specs=[
            pl.BlockSpec(memory_space=SMEM),
            pl.BlockSpec(memory_space=SMEM),
            pl.BlockSpec(memory_space=SMEM),
            pl.BlockSpec(memory_space=VMEM),
            pl.BlockSpec(memory_space=ANY),
        ],
        out_specs=pl.BlockSpec(memory_space=VMEM),
        scratch_shapes=[
            pltpu.SMEM((3, 2 * N_DOC + 1), jnp.int32),
            pltpu.VMEM((DEPTH, TILE, SKETCH), jnp.bfloat16),
            pltpu.SemaphoreType.DMA((DEPTH,)),
        ],
    )(notes, b_offsets, a_offsets, inbox, gathered)


def local(
    b_tiles,
    b_rows,
    b_cols,
    b_count,
    b_offsets,
    a_tiles,
    a_rows,
    a_tags,
    a_count,
    a_offsets,
    omega_seed,
):
    outbox = pack_stage(a_tags[:, 0], a_rows[:, 0], a_count[:, 0], a_tiles)
    inbox = lax.all_to_all(outbox, "doc", split_axis=0, concat_axis=0, tiled=True)
    partial = text_stage(b_rows[:, 0], b_cols[:, 0], b_count[:, 0], omega_seed, b_tiles)
    mine = lax.psum_scatter(partial, "feat", scatter_dimension=0, tiled=True)
    gathered = lax.all_gather(mine.astype(jnp.bfloat16), ("doc", "feat"))
    notes = inbox[:, 2 * TILE, 0:4].astype(jnp.int32).reshape(-1)
    return final_stage(
        notes,
        b_offsets,
        a_offsets,
        inbox,
        gathered.reshape(N_DOC * ROWB_MAX, TILE, SKETCH),
    )


def solution(mesh):
    return jax.shard_map(
        local,
        mesh=mesh,
        in_specs=(
            P("doc", "feat", None),
            P("doc", "feat"),
            P("doc", "feat"),
            P("doc", "feat"),
            P(),
            P("doc", "feat", None),
            P("doc", "feat"),
            P("doc", "feat"),
            P("doc", "feat"),
            P(),
            P(),
        ),
        out_specs=P(("doc", "feat"), None),
        check_vma=False,
    )
```

```python
import functools

import jax
import jax.numpy as jnp
from jax import lax
from jax.experimental import pallas as pl
from jax.experimental.pallas import tpu as pltpu
from jax.sharding import PartitionSpec as P

TILE = 128
SKETCH = 256
TERMS = 2097152
TAG_DEV = 4096
ROWB_MAX = 12
OWNED = TAG_DEV // TILE
N_DOC = 64
N_FEAT = 4
META = 16
PAGE = 2 * TILE + META
CHUNK = 16
GROUP = 4
DEPTH = 8
PAIR_MAX = 2 * ROWB_MAX
N_X = 4
N_Z = 8
N_CORE = 2
PART = 80
REST = TILE - PART
MESH = pl.DeviceIdType.MESH

VMEM = pltpu.MemorySpace.VMEM
SMEM = pltpu.MemorySpace.SMEM
ANY = pl.ANY


def shr(value, count):
    return lax.shift_right_logical(value, jnp.full(value.shape, count, jnp.int32))


def text_kernel(rows, cols, count, seed, offsets, tiles, out, base):
    step = pl.program_id(0)

    @pl.when(step == 0)
    def _():
        row_iota = lax.broadcasted_iota(jnp.int32, (TILE, SKETCH), 0)
        col_iota = lax.broadcasted_iota(jnp.int32, (TILE, SKETCH), 1)
        start = (row_iota * SKETCH + col_iota) ^ (seed[0] * 747796405)
        base[...] = start ^ shr(start, 16)
        out[...] = jnp.zeros_like(out)

    doc = lax.axis_index("doc")
    first = offsets[doc] - offsets[doc - lax.rem(doc, 2)]
    slab = lax.axis_index("feat") * (TERMS // (TILE * N_FEAT))
    used = count[0]

    def some(width, first_at, group, carry):
        products = []
        for lane in range(width):
            at = first_at + group * width + lane
            block = (cols[step * CHUNK + at] + slab) * (TILE * SKETCH)
            block = block ^ lax.shift_right_logical(block, jnp.int32(16))
            mixing = base[...] ^ block
            mixing = mixing * 2146121005
            mixing = mixing ^ shr(mixing, 15)
            mixing = mixing * -2073254261
            mixing = mixing ^ shr(mixing, 16)
            levels = (shr(mixing, 8) & 65535).astype(jnp.float32)
            panel = ((levels - 32767.5) * (3.4641016 / 65536.0)).astype(jnp.bfloat16)
            products.append(jnp.dot(tiles[at], panel, preferred_element_type=jnp.float32))
        for lane in range(width):
            at = step * CHUNK + first_at + group * width + lane
            out[rows[at] + first] += products[lane]
        return carry

    left = jnp.clip(used - step * CHUNK, 0, CHUNK)
    whole = left // GROUP
    lax.fori_loop(0, whole, functools.partial(some, GROUP, 0), 0)
    lax.fori_loop(0, left - whole * GROUP, functools.partial(some, 1, whole * GROUP), 0)


def text_stage(b_rows, b_cols, b_count, omega_seed, b_offsets, b_tiles):
    tiles_b = b_tiles.shape[0]
    return pl.pallas_call(
        text_kernel,
        out_shape=jax.ShapeDtypeStruct((PAIR_MAX, TILE, SKETCH), jnp.float32),
        grid=(tiles_b // CHUNK,),
        in_specs=[
            pl.BlockSpec(memory_space=SMEM),
            pl.BlockSpec(memory_space=SMEM),
            pl.BlockSpec(memory_space=SMEM),
            pl.BlockSpec(memory_space=SMEM),
            pl.BlockSpec(memory_space=SMEM),
            pl.BlockSpec((CHUNK, TILE, TILE), lambda i: (i, 0, 0)),
        ],
        out_specs=pl.BlockSpec((PAIR_MAX, TILE, SKETCH), lambda i: (0, 0, 0)),
        scratch_shapes=[
            pltpu.VMEM((TILE, SKETCH), jnp.int32),
        ],
        cost_estimate=pl.CostEstimate(flops=1700000000, bytes_accessed=8000000, transcendentals=0),
    )(b_rows, b_cols, b_count, omega_seed, b_offsets, b_tiles)


def pack_kernel(tags, rows, count, tiles, outbox, meta, seen, notes, sems, meta_sem):
    used = count[0]

    def clear(owner, carry):
        seen[owner] = 0
        for lane in range(4):
            notes[owner * 4 + lane] = 0
        return carry

    lax.fori_loop(0, N_DOC, clear, 0)

    def copy(at, owner, rank):
        start = pl.multiple_of(rank * TILE, TILE)
        return pltpu.make_async_copy(
            tiles.at[at], outbox.at[owner, pl.ds(start, TILE), :], sems.at[at]
        )

    def send(at, carry):
        tag = tags[at]
        owner = lax.shift_right_logical(tag, jnp.int32(7))
        rank = jnp.minimum(seen[owner], 1)
        seen[owner] = rank + 1
        notes[owner * 4 + rank * 2] = (tag & (OWNED - 1)) + 1
        notes[owner * 4 + rank * 2 + 1] = rows[at]
        copy(at, owner, rank).start()
        return carry

    lax.fori_loop(0, used, send, 0)
    lane_iota = lax.broadcasted_iota(jnp.int32, (META, TILE), 1)

    def note(owner, carry):
        value = jnp.zeros((META, TILE), jnp.int32)
        for lane in range(4):
            value = jnp.where(lane_iota == lane, notes[owner * 4 + lane], value)
        meta[owner] = value.astype(jnp.float32).astype(jnp.bfloat16)
        return carry

    lax.fori_loop(0, N_DOC, note, 0)
    last = pltpu.make_async_copy(meta, outbox.at[:, pl.ds(2 * TILE, META), :], meta_sem)
    last.start()

    def drain(at, carry):
        copy(at, 0, 0).wait()
        return carry

    lax.fori_loop(0, used, drain, 0)
    last.wait()


def pack_stage(a_tags, a_rows, a_count, a_tiles):
    tiles_a = a_tiles.shape[0]
    return pl.pallas_call(
        pack_kernel,
        out_shape=jax.ShapeDtypeStruct((N_DOC, PAGE, TILE), jnp.bfloat16),
        in_specs=[
            pl.BlockSpec(memory_space=SMEM),
            pl.BlockSpec(memory_space=SMEM),
            pl.BlockSpec(memory_space=SMEM),
            pl.BlockSpec(memory_space=VMEM),
        ],
        out_specs=pl.BlockSpec(memory_space=ANY),
        scratch_shapes=[
            pltpu.VMEM((N_DOC, META, TILE), jnp.bfloat16),
            pltpu.SMEM((N_DOC,), jnp.int32),
            pltpu.SMEM((N_DOC * 4,), jnp.int32),
            pltpu.SemaphoreType.DMA((tiles_a,)),
            pltpu.SemaphoreType.DMA,
        ],
    )(a_tags, a_rows, a_count, a_tiles)


def exchange_kernel(
    depth,
    partial,
    outbox,
    main,
    side,
    inbox,
    stage,
    own,
    core_in,
    sums,
    feat_in,
    main_own,
    side_own,
    core_sem,
    load_sem,
    feat_sem,
    place_sem,
    z_sem,
    second_sem,
    third_sem,
    pair_sem,
    across_sem,
    tiles_sem,
    keep_sem,
):
    doc = lax.axis_index("doc")
    feat = lax.axis_index("feat")
    core = lax.rem(doc, N_CORE)
    z = lax.rem(doc // N_CORE, N_Z)
    x = doc // (N_CORE * N_Z)
    lane = z * N_CORE + core

    def device(x_to, z_to, core_to, feat_to):
        return ((x_to * N_Z + z_to) * N_CORE + core_to, feat_to)

    def turn(value, step, size):
        return lax.rem(value + (step % size), size)

    sibling = device(x, z, 1 - core, feat)

    def remote(source, target, sems, to):
        return pltpu.make_async_remote_copy(
            src_ref=source,
            dst_ref=target,
            send_sem=sems[0],
            recv_sem=sems[1],
            device_id=to,
            device_id_type=MESH,
        )

    barrier = pltpu.get_barrier_semaphore()

    def greet(step, carry):
        other = lax.rem(lane + step, N_Z * N_CORE)
        pl.semaphore_signal(
            barrier, inc=1, device_id=(x * (N_Z * N_CORE) + other, feat), device_id_type=MESH
        )
        return carry

    lax.fori_loop(1, N_Z * N_CORE, greet, 0)
    for step in range(1, N_X):
        pl.semaphore_signal(
            barrier, inc=1, device_id=device(turn(x, step, N_X), z, core, feat), device_id_type=MESH
        )
    for step in range(1, N_FEAT):
        pl.semaphore_signal(
            barrier, inc=1, device_id=device(x, z, core, turn(feat, step, N_FEAT)), device_id_type=MESH
        )
    pl.semaphore_wait(barrier, N_Z * N_CORE - 1 + N_X - 1 + N_FEAT - 1)

    from_core = remote(
        partial.at[pl.ds(0, depth), 1 - core], core_in, (core_sem.at[0], core_sem.at[1]), sibling
    )
    from_core.start()
    load = pltpu.make_async_copy(partial.at[pl.ds(0, depth), core], own, load_sem)
    load.start()

    def across(step):
        to = turn(x, step, N_X)
        return remote(
            outbox.at[to], stage.at[x], (across_sem.at[0, step], across_sem.at[1, step]),
            device(to, z, core, feat),
        )

    for step in (1, 3, 2):
        across(step).start()

    load.wait()
    from_core.wait()
    for to in range(N_FEAT):
        for k in range(depth):
            sums[to, k] = own[k, to] + core_in[k, to]

    def to_feat(step):
        to = turn(feat, step, N_FEAT)
        return remote(
            sums.at[to], feat_in.at[step - 1], (feat_sem.at[0, step], feat_sem.at[1, step]),
            device(x, z, core, to),
        )

    for step in (1, 3, 2):
        to_feat(step).start()
    for step in (1, 3, 2):
        to_feat(step).wait_recv()
    for k in range(depth):
        row = ((sums[feat, k] + feat_in[0, k]) + (feat_in[1, k] + feat_in[2, k])).astype(jnp.bfloat16)
        main_own[k] = row[:PART]
        side_own[k] = row[PART:]

    place_main = pltpu.make_async_copy(main_own, main.at[core, feat, x, z], place_sem.at[0])
    place_side = pltpu.make_async_copy(side_own, side.at[core, x, feat, z], place_sem.at[1])
    place_main.start()
    place_side.start()

    upper = depth // 2

    def ring_z(way, which, step):
        sign = 1 if way == 0 else -1
        block = turn(z, -sign * (step - 1), N_Z)
        held = main.at[core, feat, x, block] if which == 0 else side.at[core, x, feat, block]
        source = held if step > 1 else (main_own if which == 0 else side_own)
        if step == N_Z // 2:
            part = pl.ds(0, upper) if way == 0 else pl.ds(upper, depth - upper)
            held = held.at[part]
            source = source.at[part]
        return remote(
            source, held, (z_sem.at[0, way, which, step], z_sem.at[1, way, which, step]),
            device(x, turn(z, sign, N_Z), core, feat),
        )

    for step in range(1, N_Z // 2 + 1):
        for way in range(2):
            for which in range(2):
                if step > 1:
                    ring_z(way, which, step - 1).wait_recv()
                ring_z(way, which, step).start()
    for way in range(2):
        for which in range(2):
            ring_z(way, which, N_Z // 2).wait_recv()
    place_main.wait()
    place_side.wait()

    half = N_Z // 2

    def ring_four(sems, at, axis, block, kind):
        way, part, hop = kind
        sign = 1 if way == 0 else -1
        if axis == 0:
            place, to = x, device(turn(x, sign, N_X), z, core, feat)
        else:
            place, to = feat, device(x, z, core, turn(feat, sign, N_FEAT))
        ref = block(turn(place, -sign * (hop - 1), 4)).at[pl.ds(part * half, half)]
        number = way * 3 + (part ^ way if hop == 1 else 2)
        return remote(ref, ref, (sems.at[0, at, number], sems.at[1, at, number]), to)

    first_kinds = ((0, 0, 1), (1, 1, 1), (0, 1, 1), (1, 0, 1))
    later_kinds = ((0, 0, 2), (1, 1, 2))

    def main_block(feat_at, x_at):
        return main.at[core, feat_at, x_at]

    def side_block(x_at, feat_at):
        return side.at[core, x_at, feat_at]

    def second(which, kind):
        if which == 0:
            return ring_four(second_sem, 0, 0, lambda i: main_block(feat, i), kind)
        return ring_four(second_sem, 1, 1, lambda i: side_block(x, i), kind)

    def third(which, step, kind):
        if which == 0:
            chunk = turn(x, step, N_X)
            return ring_four(third_sem, step, 1, lambda i: main_block(i, chunk), kind)
        chunk = turn(feat, step, N_FEAT)
        return ring_four(third_sem, 4 + step, 0, lambda i: side_block(i, chunk), kind)

    def to_sibling(which, far, step):
        if which == 0:
            ref = main_block(turn(feat, far, N_FEAT), turn(x, step, N_X))
        else:
            ref = side_block(turn(x, far, N_X), turn(feat, step, N_FEAT))
        at = which * 16 + far * 4 + step
        return remote(ref, ref, (pair_sem.at[0, at], pair_sem.at[1, at]), sibling)

    for kind in first_kinds:
        second(1, kind).start()
        second(0, kind).start()
    for kind in first_kinds:
        third(0, 0, kind).start()
        third(1, 0, kind).start()
    to_sibling(0, 0, 0).start()
    to_sibling(1, 0, 0).start()

    def tiles_to(step, source, from_x):
        other = lax.rem(lane + step, N_Z * N_CORE)
        return remote(
            source.at[other], inbox.at[from_x, lane],
            (tiles_sem.at[0, from_x, step], tiles_sem.at[1, from_x, step]),
            (x * (N_Z * N_CORE) + other, feat),
        )

    def send_tiles(source, from_x, at):
        def one(step, carry):
            tiles_to(step, source, from_x).start()
            return carry

        lax.fori_loop(1, N_Z * N_CORE, one, 0)
        pltpu.make_async_copy(source.at[lane], inbox.at[from_x, lane], keep_sem.at[at]).start()

    send_tiles(outbox.at[x], x, 0)

    def pass_on_second(which):
        for kind in later_kinds:
            way, part, _ = kind
            second(which, (way, part, 1)).wait_recv()
            second(which, kind).start()

    def finish_second(which):
        second(which, (0, 1, 1)).wait_recv()
        for kind in first_kinds:
            third(which, 3, kind).start()
        to_sibling(which, 0, 3).start()
        second(which, (1, 0, 1)).wait_recv()
        for kind in first_kinds:
            third(which, 1, kind).start()
        to_sibling(which, 0, 1).start()

    def finish_far(which):
        for kind in later_kinds:
            second(which, kind).wait_recv()
        for kind in first_kinds:
            third(which, 2, kind).start()
        to_sibling(which, 0, 2).start()

    def pass_on_third(which, step):
        for kind in later_kinds:
            way, part, _ = kind
            third(which, step, (way, part, 1)).wait_recv()
            third(which, step, kind).start()

    def finish_third(which, step):
        third(which, step, (0, 1, 1)).wait_recv()
        to_sibling(which, 3, step).start()
        third(which, step, (1, 0, 1)).wait_recv()
        to_sibling(which, 1, step).start()
        for kind in later_kinds:
            third(which, step, kind).wait_recv()
        to_sibling(which, 2, step).start()

    pass_on_second(1)
    pass_on_second(0)
    finish_second(1)
    pass_on_third(1, 0)
    pass_on_third(0, 0)
    finish_second(0)
    finish_far(1)
    finish_far(0)
    for at, step in ((1, 1), (2, 3), (3, 2)):
        across(step).wait_recv()
        from_x = turn(x, -step, N_X)
        send_tiles(stage.at[from_x], from_x, at)
    finish_third(1, 0)
    finish_third(0, 0)
    for step in (3, 1, 2):
        pass_on_third(1, step)
        pass_on_third(0, step)
        finish_third(1, step)
        finish_third(0, step)

    for which in range(2):
        for far in range(4):
            for step in range(4):
                to_sibling(which, far, step).wait_recv()
                to_sibling(which, far, step).wait_send()
        for kind in first_kinds + later_kinds:
            second(which, kind).wait_send()
        for step in range(4):
            for kind in first_kinds + later_kinds:
                third(which, step, kind).wait_send()
        for way in range(2):
            for step in range(1, N_Z // 2 + 1):
                ring_z(way, which, step).wait_send()
    for step in (1, 2, 3):
        to_feat(step).wait_send()
        across(step).wait_send()

    def settle(from_x, carry):
        def one(step, inner):
            copy = tiles_to(step, stage.at[0], from_x)
            copy.wait_recv()
            copy.wait_send()
            return inner

        lax.fori_loop(1, N_Z * N_CORE, one, 0)
        pltpu.make_async_copy(stage.at[0, 0], inbox.at[0, 0], keep_sem.at[from_x]).wait()
        return carry

    lax.fori_loop(0, N_X, settle, 0)


def exchange_stage(depth, partial, outbox):
    bf16 = jnp.bfloat16
    dma = pltpu.SemaphoreType.DMA
    wide = N_Z * N_CORE
    block = (TILE, SKETCH)
    main, side, inbox, _ = pl.pallas_call(
        functools.partial(exchange_kernel, depth),
        out_shape=(
            jax.ShapeDtypeStruct((N_CORE, N_FEAT, N_X, N_Z, depth, PART, SKETCH), bf16),
            jax.ShapeDtypeStruct((N_CORE, N_X, N_FEAT, N_Z, depth, REST, SKETCH), bf16),
            jax.ShapeDtypeStruct((N_X, wide, PAGE, TILE), bf16),
            jax.ShapeDtypeStruct((N_X, wide, PAGE, TILE), bf16),
        ),
        in_specs=[pl.BlockSpec(memory_space=ANY)] * 2,
        out_specs=(pl.BlockSpec(memory_space=ANY),) * 4,
        scratch_shapes=[
            pltpu.VMEM((depth, N_FEAT) + block, jnp.float32),
            pltpu.VMEM((depth, N_FEAT) + block, jnp.float32),
            pltpu.VMEM((N_FEAT, depth) + block, jnp.float32),
            pltpu.VMEM((N_FEAT - 1, depth) + block, jnp.float32),
            pltpu.VMEM((depth, PART, SKETCH), bf16),
            pltpu.VMEM((depth, REST, SKETCH), bf16),
            dma((2,)),
            dma,
            dma((2, 4)),
            dma((2,)),
            dma((2, 2, 2, N_Z // 2 + 1)),
            dma((2, 2, 6)),
            dma((2, 8, 6)),
            dma((2, 32)),
            dma((2, 4)),
            dma((2, N_X, wide)),
            dma((4,)),
        ],
        compiler_params=pltpu.CompilerParams(collective_id=depth, has_side_effects=True),
        name="exchange_%d" % depth,
    )(
        partial.reshape(PAIR_MAX // 8, N_CORE, N_FEAT, TILE, SKETCH),
        outbox.reshape(N_X, wide, PAGE, TILE),
    )
    count = N_CORE * N_FEAT * N_X * N_Z * depth
    return (
        main.reshape(count, PART, SKETCH),
        side.reshape(count, REST, SKETCH),
        inbox.reshape(N_DOC, PAGE, TILE),
    )


def final_kernel(
    depth, notes, b_offsets, a_offsets, inbox, main, side, out, lists, zbuf, main_sems, side_sems
):
    def listed(doc, found):
        for rank in range(2):
            tag = notes[doc * 4 + rank * 2] - 1
            row = notes[doc * 4 + rank * 2 + 1] + a_offsets[doc]
            owner = jnp.maximum(doc - (row < b_offsets[doc]).astype(jnp.int32), 0)
            chip = lax.shift_right_logical(owner, jnp.int32(1))
            inner = jnp.clip(row - b_offsets[chip * 2], 0, depth * 8 - 1)
            k = lax.shift_right_logical(inner, jnp.int32(3))
            core = lax.shift_right_logical(inner, jnp.int32(2)) & 1
            feat = inner & 3
            x = lax.shift_right_logical(chip, jnp.int32(3))
            z = chip & 7
            lists[0, found] = tag
            lists[1, found] = (((core * N_FEAT + feat) * N_X + x) * N_Z + z) * depth + k
            lists[2, found] = (((core * N_X + x) * N_FEAT + feat) * N_Z + z) * depth + k
            lists[3, found] = doc * 2 + rank
            found = found + (tag >= 0).astype(jnp.int32)
        return found

    total = lax.fori_loop(0, N_DOC, listed, 0)

    def fetch(at, slot):
        return (
            pltpu.make_async_copy(
                main.at[lists[1, at]], zbuf.at[slot, pl.ds(0, PART)], main_sems.at[slot]
            ),
            pltpu.make_async_copy(
                side.at[lists[2, at]], zbuf.at[slot, pl.ds(PART, REST)], side_sems.at[slot]
            ),
        )

    for first in range(DEPTH):

        @pl.when(first < total)
        def _():
            for copy in fetch(first, first):
                copy.start()

    out[...] = jnp.zeros_like(out)

    def add(at, carry):
        slot = lax.rem(at, DEPTH)
        for copy in fetch(at, slot):
            copy.wait()
        source = lists[3, at]
        start = pl.multiple_of((source & 1) * TILE, TILE)
        tile = inbox[lax.shift_right_logical(source, jnp.int32(1)), pl.ds(start, TILE), :]
        product = lax.dot_general(
            tile, zbuf[slot], (((0,), (0,)), ((), ())), preferred_element_type=jnp.float32
        )
        place = pl.multiple_of(lists[0, at] * TILE, TILE)
        out[pl.ds(place, TILE), :] += product

        @pl.when(at + DEPTH < total)
        def _():
            for copy in fetch(at + DEPTH, slot):
                copy.start()

        return carry

    lax.fori_loop(0, total, add, 0)


def final_stage(depth, notes, b_offsets, a_offsets, inbox, main, side):
    return pl.pallas_call(
        functools.partial(final_kernel, depth),
        out_shape=jax.ShapeDtypeStruct((TAG_DEV, SKETCH), jnp.float32),
        in_specs=[
            pl.BlockSpec(memory_space=SMEM),
            pl.BlockSpec(memory_space=SMEM),
            pl.BlockSpec(memory_space=SMEM),
            pl.BlockSpec(memory_space=VMEM),
            pl.BlockSpec(memory_space=ANY),
            pl.BlockSpec(memory_space=ANY),
        ],
        out_specs=pl.BlockSpec(memory_space=VMEM),
        scratch_shapes=[
            pltpu.SMEM((4, 2 * N_DOC + 1), jnp.int32),
            pltpu.VMEM((DEPTH, TILE, SKETCH), jnp.bfloat16),
            pltpu.SemaphoreType.DMA((DEPTH,)),
            pltpu.SemaphoreType.DMA((DEPTH,)),
        ],
    )(notes, b_offsets, a_offsets, inbox, main, side)


def local(
    b_tiles,
    b_rows,
    b_cols,
    b_count,
    b_offsets,
    a_tiles,
    a_rows,
    a_tags,
    a_count,
    a_offsets,
    omega_seed,
):
    outbox = pack_stage(a_tags[:, 0], a_rows[:, 0], a_count[:, 0], a_tiles)
    partial = text_stage(b_rows[:, 0], b_cols[:, 0], b_count[:, 0], omega_seed, b_offsets, b_tiles)

    def rest(depth, partial, outbox):
        main, side, inbox = exchange_stage(depth, partial, outbox)
        notes = inbox[:, 2 * TILE, 0:4].astype(jnp.int32).reshape(-1)
        return final_stage(depth, notes, b_offsets, a_offsets, inbox, main, side)

    most = jnp.max(b_offsets[2::2] - b_offsets[:-1:2])
    return lax.cond(
        most <= 16, functools.partial(rest, 2), functools.partial(rest, 3), partial, outbox
    )


def solution(mesh):
    return jax.shard_map(
        local,
        mesh=mesh,
        in_specs=(
            P("doc", "feat", None),
            P("doc", "feat"),
            P("doc", "feat"),
            P("doc", "feat"),
            P(),
            P("doc", "feat", None),
            P("doc", "feat"),
            P("doc", "feat"),
            P("doc", "feat"),
            P(),
            P(),
        ),
        out_specs=P(("doc", "feat"), None),
        check_vma=False,
    )
```

```python
import functools

import jax
import jax.numpy as jnp
from jax import lax
from jax.experimental import pallas as pl
from jax.experimental.pallas import tpu as pltpu
from jax.sharding import PartitionSpec as P

TILE = 128
SKETCH = 256
TERMS = 2097152
TAG_DEV = 4096
ROWB_MAX = 12
OWNED = TAG_DEV // TILE
N_DOC = 64
N_FEAT = 4
META = 16
PAGE = 2 * TILE + META
CHUNK = 16
GROUP = 4
TOGETHER = 4
DEPTH = 2 * N_DOC
PAIR_MAX = 2 * ROWB_MAX
N_X = 4
N_Z = 8
N_CORE = 2
MESH = pl.DeviceIdType.MESH

VMEM = pltpu.MemorySpace.VMEM
SMEM = pltpu.MemorySpace.SMEM
ANY = pl.ANY


def shr(value, count):
    return lax.shift_right_logical(value, jnp.full(value.shape, count, jnp.int32))


def text_kernel(
    rows, cols, count, seed, offsets, tags, tag_rows, tag_count, tiles, tag_tiles,
    out, outbox,
    acc, base, held, meta, seen, notes, slots, load_sem, sems, meta_sem,
):
    step = pl.program_id(0)
    used_tags = tag_count[0]

    def load():
        return pltpu.make_async_copy(tag_tiles, held, load_sem)

    def put(at, owner, rank):
        start = pl.multiple_of(rank * TILE, TILE)
        return pltpu.make_async_copy(
            held.at[at], outbox.at[owner, pl.ds(start, TILE), :], sems.at[at]
        )

    def put_meta():
        return pltpu.make_async_copy(meta, outbox.at[:, pl.ds(2 * TILE, META), :], meta_sem)

    @pl.when(step == 0)
    def _():
        load().start()
        row_iota = lax.broadcasted_iota(jnp.int32, (TILE, SKETCH), 0)
        col_iota = lax.broadcasted_iota(jnp.int32, (TILE, SKETCH), 1)
        start = (row_iota * SKETCH + col_iota) ^ (seed[0] * 747796405)
        base[...] = start ^ shr(start, 16)
        acc[...] = jnp.zeros_like(acc)

        def clear(owner, carry):
            seen[owner] = 0
            for lane in range(4):
                notes[owner * 4 + lane] = 0
            return carry

        lax.fori_loop(0, N_DOC, clear, 0)

        def sort(at, carry):
            tag = tags[at]
            owner = lax.shift_right_logical(tag, jnp.int32(7))
            rank = jnp.minimum(seen[owner], 1)
            seen[owner] = rank + 1
            notes[owner * 4 + rank * 2] = (tag & (OWNED - 1)) + 1
            notes[owner * 4 + rank * 2 + 1] = tag_rows[at]
            slots[at] = owner * 2 + rank
            return carry

        lax.fori_loop(0, used_tags, sort, 0)

    @pl.when(step == 1)
    def _():
        load().wait()

        def send(at, carry):
            slot = slots[at]
            put(at, lax.shift_right_logical(slot, jnp.int32(1)), slot & 1).start()
            return carry

        lax.fori_loop(0, used_tags, send, 0)
        lane_iota = lax.broadcasted_iota(jnp.int32, (META, TILE), 1)

        def note(owner, carry):
            value = jnp.zeros((META, TILE), jnp.int32)
            for lane in range(4):
                value = jnp.where(lane_iota == lane, notes[owner * 4 + lane], value)
            meta[owner] = value.astype(jnp.float32).astype(jnp.bfloat16)
            return carry

        lax.fori_loop(0, N_DOC, note, 0)
        put_meta().start()

    doc = lax.axis_index("doc")
    first = offsets[doc] - offsets[doc - lax.rem(doc, 2)]
    slab = lax.axis_index("feat") * (TERMS // (TILE * N_FEAT))
    used = count[0]

    def some(width, first_at, group, carry):
        products = []
        for lane in range(width):
            at = first_at + group * width + lane
            block = (cols[step * CHUNK + at] + slab) * (TILE * SKETCH)
            block = block ^ lax.shift_right_logical(block, jnp.int32(16))
            mixing = base[...] ^ block
            mixing = mixing * 2146121005
            mixing = mixing ^ shr(mixing, 15)
            mixing = mixing * -2073254261
            mixing = mixing ^ shr(mixing, 16)
            levels = (shr(mixing, 8) & 65535).astype(jnp.float32)
            panel = ((levels - 32767.5) * (3.4641016 / 65536.0)).astype(jnp.bfloat16)
            products.append(jnp.dot(tiles[at], panel, preferred_element_type=jnp.float32))
        for lane in range(width):
            at = step * CHUNK + first_at + group * width + lane
            acc[rows[at] + first] += products[lane]
        return carry

    left = jnp.clip(used - step * CHUNK, 0, CHUNK)
    whole = left // GROUP
    lax.fori_loop(0, whole, functools.partial(some, GROUP, 0), 0)
    lax.fori_loop(0, left - whole * GROUP, functools.partial(some, 1, whole * GROUP), 0)

    @pl.when(step == pl.num_programs(0) - 1)
    def _():
        out[...] = acc[...].astype(jnp.bfloat16)

        def drain(at, carry):
            put(at, 0, 0).wait()
            return carry

        lax.fori_loop(0, used_tags, drain, 0)
        put_meta().wait()


def text_stage(b_rows, b_cols, b_count, omega_seed, b_offsets, a_tags, a_rows, a_count, b_tiles, a_tiles):
    tiles_b, tiles_a = b_tiles.shape[0], a_tiles.shape[0]
    rows_shape = (PAIR_MAX, TILE, SKETCH)
    return pl.pallas_call(
        text_kernel,
        out_shape=(
            jax.ShapeDtypeStruct(rows_shape, jnp.bfloat16),
            jax.ShapeDtypeStruct((N_DOC, PAGE, TILE), jnp.bfloat16),
        ),
        grid=(tiles_b // CHUNK,),
        in_specs=[pl.BlockSpec(memory_space=SMEM)] * 8
        + [
            pl.BlockSpec((CHUNK, TILE, TILE), lambda i: (i, 0, 0)),
            pl.BlockSpec(memory_space=ANY),
        ],
        out_specs=(
            pl.BlockSpec(rows_shape, lambda i: (0, 0, 0)),
            pl.BlockSpec(memory_space=ANY),
        ),
        scratch_shapes=[
            pltpu.VMEM(rows_shape, jnp.float32),
            pltpu.VMEM((TILE, SKETCH), jnp.int32),
            pltpu.VMEM((tiles_a, TILE, TILE), jnp.bfloat16),
            pltpu.VMEM((N_DOC, META, TILE), jnp.bfloat16),
            pltpu.SMEM((N_DOC,), jnp.int32),
            pltpu.SMEM((N_DOC * 4,), jnp.int32),
            pltpu.SMEM((tiles_a,), jnp.int32),
            pltpu.SemaphoreType.DMA,
            pltpu.SemaphoreType.DMA((tiles_a,)),
            pltpu.SemaphoreType.DMA,
        ],
        cost_estimate=pl.CostEstimate(flops=1700000000, bytes_accessed=8000000, transcendentals=0),
        name="text",
    )(b_rows, b_cols, b_count, omega_seed, b_offsets, a_tags, a_rows, a_count, b_tiles, a_tiles)


def exchange_kernel(
    depth,
    partial,
    outbox,
    main,
    side,
    inbox,
    stage,
    own,
    core_in,
    sums,
    feat_in,
    main_own,
    side_own,
    core_sem,
    load_sem,
    feat_sem,
    place_sem,
    z_sem,
    second_sem,
    third_sem,
    pair_sem,
    across_sem,
    tiles_sem,
    keep_sem,
):
    count = main.shape[4]
    doc = lax.axis_index("doc")
    feat = lax.axis_index("feat")
    core = lax.rem(doc, N_CORE)
    z = lax.rem(doc // N_CORE, N_Z)
    x = doc // (N_CORE * N_Z)
    lane = z * N_CORE + core

    def device(x_to, z_to, core_to, feat_to):
        return ((x_to * N_Z + z_to) * N_CORE + core_to, feat_to)

    def turn(value, step, size):
        return lax.rem(value + (step % size), size)

    sibling = device(x, z, 1 - core, feat)

    def remote(source, target, sems, to):
        return pltpu.make_async_remote_copy(
            src_ref=source,
            dst_ref=target,
            send_sem=sems[0],
            recv_sem=sems[1],
            device_id=to,
            device_id_type=MESH,
        )

    barrier = pltpu.get_barrier_semaphore()

    def greet(step, carry):
        other = lax.rem(lane + step, N_Z * N_CORE)
        pl.semaphore_signal(
            barrier, inc=1, device_id=(x * (N_Z * N_CORE) + other, feat), device_id_type=MESH
        )
        return carry

    lax.fori_loop(1, N_Z * N_CORE, greet, 0)
    for step in range(1, N_X):
        pl.semaphore_signal(
            barrier, inc=1, device_id=device(turn(x, step, N_X), z, core, feat), device_id_type=MESH
        )
    for step in range(1, N_FEAT):
        pl.semaphore_signal(
            barrier, inc=1, device_id=device(x, z, core, turn(feat, step, N_FEAT)), device_id_type=MESH
        )
    pl.semaphore_wait(barrier, N_Z * N_CORE - 1 + N_X - 1 + N_FEAT - 1)

    from_core = remote(
        partial.at[pl.ds(0, depth), 1 - core], core_in, (core_sem.at[0], core_sem.at[1]), sibling
    )
    from_core.start()
    load = pltpu.make_async_copy(partial.at[pl.ds(0, depth), core], own, load_sem)
    load.start()

    def across(step):
        to = turn(x, step, N_X)
        return remote(
            outbox.at[to], stage.at[x], (across_sem.at[0, step], across_sem.at[1, step]),
            device(to, z, core, feat),
        )

    for step in (1, 3, 2):
        across(step).start()

    def tiles_to(step, source, from_x):
        other = lax.rem(lane + step, N_Z * N_CORE)
        return remote(
            source.at[other], inbox.at[from_x, lane],
            (tiles_sem.at[0, from_x, step], tiles_sem.at[1, from_x, step]),
            (x * (N_Z * N_CORE) + other, feat),
        )

    def send_tiles(source, from_x, at):
        def one(step, carry):
            tiles_to(step, source, from_x).start()
            return carry

        lax.fori_loop(1, N_Z * N_CORE, one, 0)
        pltpu.make_async_copy(source.at[lane], inbox.at[from_x, lane], keep_sem.at[at]).start()

    send_tiles(outbox.at[x], x, 0)

    load.wait()
    from_core.wait()
    for to in range(N_FEAT):
        for k in range(depth):
            sums[to, k] = own[k, to] + core_in[k, to]

    def to_feat(step):
        to = turn(feat, step, N_FEAT)
        return remote(
            sums.at[to], feat_in.at[step - 1], (feat_sem.at[0, step], feat_sem.at[1, step]),
            device(x, z, core, to),
        )

    for step in (1, 3, 2):
        to_feat(step).start()
    for step in (1, 3, 2):
        to_feat(step).wait_recv()
    for k in range(depth):
        terms = [block[k].astype(jnp.float32) for block in (sums.at[feat], feat_in.at[0], feat_in.at[1], feat_in.at[2])]
        row = ((terms[0] + terms[1]) + (terms[2] + terms[3])).astype(jnp.bfloat16)
        if k < count:
            main_own[k] = row
        else:
            side_own[k - count] = row

    place_main = pltpu.make_async_copy(main_own, main.at[core, feat, x, z], place_sem.at[0])
    place_side = pltpu.make_async_copy(side_own, side.at[core, x, feat, z], place_sem.at[1])
    place_main.start()
    place_side.start()

    upper = TILE // 2

    def ring_z(way, which, step):
        sign = 1 if way == 0 else -1
        block = turn(z, -sign * (step - 1), N_Z)
        held = main.at[core, feat, x, block] if which == 0 else side.at[core, x, feat, block]
        source = held if step > 1 else (main_own if which == 0 else side_own)
        if step == N_Z // 2:
            part = pl.ds(way * upper, upper)
            held = held.at[:, part]
            source = source.at[:, part]
        return remote(
            source, held, (z_sem.at[0, way, which, step], z_sem.at[1, way, which, step]),
            device(x, turn(z, sign, N_Z), core, feat),
        )

    for step in range(1, N_Z // 2 + 1):
        for way in range(2):
            for which in range(2):
                if step > 1:
                    ring_z(way, which, step - 1).wait_recv()
                ring_z(way, which, step).start()
    for way in range(2):
        for which in range(2):
            ring_z(way, which, N_Z // 2).wait_recv()
    place_main.wait()
    place_side.wait()

    half = N_Z // 2

    def ring_four(sems, at, axis, block, kind):
        way, part, hop = kind
        sign = 1 if way == 0 else -1
        if axis == 0:
            place, to = x, device(turn(x, sign, N_X), z, core, feat)
        else:
            place, to = feat, device(x, z, core, turn(feat, sign, N_FEAT))
        ref = block(turn(place, -sign * (hop - 1), 4)).at[pl.ds(part * half, half)]
        number = way * 3 + (part ^ way if hop == 1 else 2)
        return remote(ref, ref, (sems.at[0, at, number], sems.at[1, at, number]), to)

    first_kinds = ((0, 0, 1), (1, 1, 1), (0, 1, 1), (1, 0, 1))
    later_kinds = ((0, 0, 2), (1, 1, 2))

    def main_block(feat_at, x_at):
        return main.at[core, feat_at, x_at]

    def side_block(x_at, feat_at):
        return side.at[core, x_at, feat_at]

    def second(which, kind):
        if which == 0:
            return ring_four(second_sem, 0, 0, lambda i: main_block(feat, i), kind)
        return ring_four(second_sem, 1, 1, lambda i: side_block(x, i), kind)

    def third(which, step, kind):
        if which == 0:
            chunk = turn(x, step, N_X)
            return ring_four(third_sem, step, 1, lambda i: main_block(i, chunk), kind)
        chunk = turn(feat, step, N_FEAT)
        return ring_four(third_sem, 4 + step, 0, lambda i: side_block(i, chunk), kind)

    def to_sibling(which, far, step):
        if which == 0:
            ref = main_block(turn(feat, far, N_FEAT), turn(x, step, N_X))
        else:
            ref = side_block(turn(x, far, N_X), turn(feat, step, N_FEAT))
        at = which * 16 + far * 4 + step
        return remote(ref, ref, (pair_sem.at[0, at], pair_sem.at[1, at]), sibling)

    for kind in first_kinds:
        second(1, kind).start()
        second(0, kind).start()
    for kind in first_kinds:
        third(0, 0, kind).start()
        third(1, 0, kind).start()
    to_sibling(0, 0, 0).start()
    to_sibling(1, 0, 0).start()

    def pass_on_second(which):
        for kind in later_kinds:
            way, part, _ = kind
            second(which, (way, part, 1)).wait_recv()
            second(which, kind).start()

    def finish_second(which):
        second(which, (0, 1, 1)).wait_recv()
        for kind in first_kinds:
            third(which, 3, kind).start()
        to_sibling(which, 0, 3).start()
        second(which, (1, 0, 1)).wait_recv()
        for kind in first_kinds:
            third(which, 1, kind).start()
        to_sibling(which, 0, 1).start()

    def finish_far(which):
        for kind in later_kinds:
            second(which, kind).wait_recv()
        for kind in first_kinds:
            third(which, 2, kind).start()
        to_sibling(which, 0, 2).start()

    def pass_on_third(which, step):
        for kind in later_kinds:
            way, part, _ = kind
            third(which, step, (way, part, 1)).wait_recv()
            third(which, step, kind).start()

    def finish_third(which, step):
        third(which, step, (0, 1, 1)).wait_recv()
        to_sibling(which, 3, step).start()
        third(which, step, (1, 0, 1)).wait_recv()
        to_sibling(which, 1, step).start()
        for kind in later_kinds:
            third(which, step, kind).wait_recv()
        to_sibling(which, 2, step).start()

    def send_across(at, step):
        across(step).wait_recv()
        from_x = turn(x, -step, N_X)
        send_tiles(stage.at[from_x], from_x, at)

    pass_on_second(1)
    pass_on_second(0)
    send_across(1, 1)
    send_across(2, 3)
    finish_second(1)
    finish_second(0)
    pass_on_third(1, 0)
    pass_on_third(0, 0)
    send_across(3, 2)
    finish_far(1)
    finish_far(0)
    finish_third(1, 0)
    finish_third(0, 0)
    for step in (3, 1, 2):
        pass_on_third(1, step)
        pass_on_third(0, step)
        finish_third(1, step)
        finish_third(0, step)

    for which in range(2):
        for far in range(4):
            for step in range(4):
                to_sibling(which, far, step).wait_recv()
                to_sibling(which, far, step).wait_send()
        for kind in first_kinds + later_kinds:
            second(which, kind).wait_send()
        for step in range(4):
            for kind in first_kinds + later_kinds:
                third(which, step, kind).wait_send()
        for way in range(2):
            for step in range(1, N_Z // 2 + 1):
                ring_z(way, which, step).wait_send()
    for step in (1, 2, 3):
        to_feat(step).wait_send()
        across(step).wait_send()

    def settle(from_x, carry):
        def one(step, inner):
            copy = tiles_to(step, stage.at[0], from_x)
            copy.wait_recv()
            copy.wait_send()
            return inner

        lax.fori_loop(1, N_Z * N_CORE, one, 0)
        pltpu.make_async_copy(stage.at[0, 0], inbox.at[0, 0], keep_sem.at[from_x]).wait()
        return carry

    lax.fori_loop(0, N_X, settle, 0)


def exchange_stage(depth, partial, outbox):
    bf16 = jnp.bfloat16
    dma = pltpu.SemaphoreType.DMA
    wide = N_Z * N_CORE
    block = (TILE, SKETCH)
    first = (depth + 1) // 2
    main, side, inbox, _ = pl.pallas_call(
        functools.partial(exchange_kernel, depth),
        out_shape=(
            jax.ShapeDtypeStruct((N_CORE, N_FEAT, N_X, N_Z, first) + block, bf16),
            jax.ShapeDtypeStruct((N_CORE, N_X, N_FEAT, N_Z, depth - first) + block, bf16),
            jax.ShapeDtypeStruct((N_X, wide, PAGE, TILE), bf16),
            jax.ShapeDtypeStruct((N_X, wide, PAGE, TILE), bf16),
        ),
        in_specs=[pl.BlockSpec(memory_space=ANY)] * 2,
        out_specs=(pl.BlockSpec(memory_space=ANY),) * 4,
        scratch_shapes=[
            pltpu.VMEM((depth, N_FEAT) + block, bf16),
            pltpu.VMEM((depth, N_FEAT) + block, bf16),
            pltpu.VMEM((N_FEAT, depth) + block, bf16),
            pltpu.VMEM((N_FEAT - 1, depth) + block, bf16),
            pltpu.VMEM((first,) + block, bf16),
            pltpu.VMEM((depth - first,) + block, bf16),
            dma((2,)),
            dma,
            dma((2, 4)),
            dma((2,)),
            dma((2, 2, 2, N_Z // 2 + 1)),
            dma((2, 2, 6)),
            dma((2, 8, 6)),
            dma((2, 32)),
            dma((2, 4)),
            dma((2, N_X, wide)),
            dma((4,)),
        ],
        compiler_params=pltpu.CompilerParams(collective_id=depth, has_side_effects=True),
        name="exchange_%d" % depth,
    )(
        partial.reshape(PAIR_MAX // 8, N_CORE, N_FEAT, TILE, SKETCH),
        outbox.reshape(N_X, wide, PAGE, TILE),
    )
    return (
        main.reshape((-1,) + block),
        side.reshape((-1,) + block),
        inbox.reshape(N_DOC, PAGE, TILE),
    )


def final_kernel(
    depth, notes, b_offsets, a_offsets, inbox, main, side, out, lists, zbuf, sems
):
    first_count = (depth + 1) // 2

    def fetch(ref, at, slot):
        group = lax.shift_right_logical(slot, jnp.int32(2))
        return pltpu.make_async_copy(ref.at[at], zbuf.at[slot], sems.at[group])

    def listed(doc, found):
        shift = a_offsets[doc]
        split = b_offsets[doc]
        before = jnp.maximum(doc - 1, 0)
        chips = [lax.shift_right_logical(at, jnp.int32(1)) for at in (before, doc)]
        bases = [shift - b_offsets[chip * 2] for chip in chips]
        for rank in range(2):
            tag = notes[doc * 4 + rank * 2] - 1

            @pl.when(tag >= 0)
            def _():
                row = notes[doc * 4 + rank * 2 + 1]
                early = row + shift < split
                chip = jnp.where(early, chips[0], chips[1])
                inner = jnp.clip(row + jnp.where(early, bases[0], bases[1]), 0, depth * 8 - 1)
                k = lax.shift_right_logical(inner, jnp.int32(3))
                core = lax.shift_right_logical(inner, jnp.int32(2)) & 1
                feat = inner & 3
                x = lax.shift_right_logical(chip, jnp.int32(3))
                z = chip & 7
                lists[0, found] = tag
                lists[1, found] = doc * 2 + rank

                @pl.when(k < first_count)
                def _():
                    at = (((core * N_FEAT + feat) * N_X + x) * N_Z + z) * first_count + k
                    fetch(main, at, found).start()

                @pl.when(k >= first_count)
                def _():
                    at = (((core * N_X + x) * N_FEAT + feat) * N_Z + z) * (
                        depth - first_count
                    ) + (k - first_count)
                    fetch(side, at, found).start()

            found = found + (tag >= 0).astype(jnp.int32)
        return found

    total = lax.fori_loop(0, N_DOC, listed, 0)
    groups = (total + TOGETHER - 1) // TOGETHER

    def fill(at, carry):
        lists[0, at] = 0
        lists[1, at] = 0
        fetch(main, 0, at).start()
        return carry

    lax.fori_loop(total, groups * TOGETHER, fill, 0)
    out[...] = jnp.zeros_like(out)

    def add(group, carry):
        first = group * TOGETHER
        pltpu.make_async_copy(
            main.at[pl.ds(0, TOGETHER)], zbuf.at[pl.ds(first, TOGETHER)], sems.at[group]
        ).wait()
        products = []
        for lane in range(TOGETHER):
            at = first + lane
            source = lists[1, at]
            start = pl.multiple_of((source & 1) * TILE, TILE)
            tile = inbox[lax.shift_right_logical(source, jnp.int32(1)), pl.ds(start, TILE), :]
            product = lax.dot_general(
                tile, zbuf[at], (((0,), (0,)), ((), ())), preferred_element_type=jnp.float32
            )
            products.append(jnp.where(at < total, product, 0.0))
        for lane in range(TOGETHER):
            place = pl.multiple_of(lists[0, first + lane] * TILE, TILE)
            out[pl.ds(place, TILE), :] += products[lane]
        return carry

    lax.fori_loop(0, groups, add, 0)


def final_stage(depth, notes, b_offsets, a_offsets, inbox, main, side):
    return pl.pallas_call(
        functools.partial(final_kernel, depth),
        out_shape=jax.ShapeDtypeStruct((TAG_DEV, SKETCH), jnp.float32),
        in_specs=[
            pl.BlockSpec(memory_space=SMEM),
            pl.BlockSpec(memory_space=SMEM),
            pl.BlockSpec(memory_space=SMEM),
            pl.BlockSpec(memory_space=VMEM),
            pl.BlockSpec(memory_space=ANY),
            pl.BlockSpec(memory_space=ANY),
        ],
        out_specs=pl.BlockSpec(memory_space=VMEM),
        scratch_shapes=[
            pltpu.SMEM((2, DEPTH), jnp.int32),
            pltpu.VMEM((DEPTH, TILE, SKETCH), jnp.bfloat16),
            pltpu.SemaphoreType.DMA((DEPTH // TOGETHER,)),
        ],
    )(notes, b_offsets, a_offsets, inbox, main, side)


def local(
    b_tiles,
    b_rows,
    b_cols,
    b_count,
    b_offsets,
    a_tiles,
    a_rows,
    a_tags,
    a_count,
    a_offsets,
    omega_seed,
):
    partial, outbox = text_stage(
        b_rows[:, 0],
        b_cols[:, 0],
        b_count[:, 0],
        omega_seed,
        b_offsets,
        a_tags[:, 0],
        a_rows[:, 0],
        a_count[:, 0],
        b_tiles,
        a_tiles,
    )

    def rest(depth, partial, outbox):
        main, side, inbox = exchange_stage(depth, partial, outbox)
        notes = inbox[:, 2 * TILE, 0:4].astype(jnp.int32).reshape(-1)
        return final_stage(depth, notes, b_offsets, a_offsets, inbox, main, side)

    most = jnp.max(b_offsets[2::2] - b_offsets[:-1:2])
    return lax.cond(
        most <= 16, functools.partial(rest, 2), functools.partial(rest, 3), partial, outbox
    )


def solution(mesh):
    return jax.shard_map(
        local,
        mesh=mesh,
        in_specs=(
            P("doc", "feat", None),
            P("doc", "feat"),
            P("doc", "feat"),
            P("doc", "feat"),
            P(),
            P("doc", "feat", None),
            P("doc", "feat"),
            P("doc", "feat"),
            P("doc", "feat"),
            P(),
            P(),
        ),
        out_specs=P(("doc", "feat"), None),
        check_vma=False,
    )
```

```python
import functools

import jax
import jax.numpy as jnp
from jax import lax
from jax.experimental import pallas as pl
from jax.experimental.pallas import tpu as pltpu
from jax.sharding import PartitionSpec as P

TILE = 128
SKETCH = 256
TERMS = 2097152
TAG_DEV = 4096
ROWB_MAX = 12
OWNED = TAG_DEV // TILE
N_DOC = 64
N_FEAT = 4
META = 16
PAGE = 2 * TILE + META
CHUNK = 16
GROUP = 4
TOGETHER = 4
DEPTH = 2 * N_DOC
PAIR_MAX = 2 * ROWB_MAX
N_X = 4
N_Z = 8
N_CORE = 2
WIDE = N_Z * N_CORE
MESH = pl.DeviceIdType.MESH

VMEM = pltpu.MemorySpace.VMEM
SMEM = pltpu.MemorySpace.SMEM
ANY = pl.ANY


def shr(value, count):
    return lax.shift_right_logical(value, jnp.full(value.shape, count, jnp.int32))


def pack_kernel(tags, tag_rows, count, tiles, *refs):
    outs = refs[:N_X]
    meta, seen, notes, sems, meta_sems = refs[N_X:]
    used = count[0]
    x = lax.axis_index("doc") // WIDE

    def clear(owner, carry):
        seen[owner] = 0
        for lane in range(4):
            notes[owner * 4 + lane] = 0
        return carry

    lax.fori_loop(0, N_DOC, clear, 0)

    def put(at, step, lane, rank):
        start = pl.multiple_of(rank * TILE, TILE)
        return pltpu.make_async_copy(
            tiles.at[at], outs[step].at[lane, pl.ds(start, TILE), :], sems.at[at]
        )

    def send(at, carry):
        tag = tags[at]
        owner = lax.shift_right_logical(tag, jnp.int32(7))
        rank = jnp.minimum(seen[owner], 1)
        seen[owner] = rank + 1
        notes[owner * 4 + rank * 2] = (tag & (OWNED - 1)) + 1
        notes[owner * 4 + rank * 2 + 1] = tag_rows[at]
        away = (lax.shift_right_logical(owner, jnp.int32(4)) - x) & (N_X - 1)
        for step in range(N_X):

            @pl.when(away == step)
            def _():
                put(at, step, owner & (WIDE - 1), rank).start()

        return carry

    lax.fori_loop(0, used, send, 0)
    lane_iota = lax.broadcasted_iota(jnp.int32, (META, TILE), 1)

    def note(owner, carry):
        value = jnp.zeros((META, TILE), jnp.int32)
        for lane in range(4):
            value = jnp.where(lane_iota == lane, notes[owner * 4 + lane], value)
        meta[owner] = value.astype(jnp.float32).astype(jnp.bfloat16)
        return carry

    lax.fori_loop(0, N_DOC, note, 0)

    def put_meta(step):
        start = lax.rem(x + step, N_X) * WIDE
        return pltpu.make_async_copy(
            meta.at[pl.ds(start, WIDE)],
            outs[step].at[:, pl.ds(2 * TILE, META), :],
            meta_sems.at[step],
        )

    for step in range(N_X):
        put_meta(step).start()

    def drain(at, carry):
        put(at, 0, 0, 0).wait()
        return carry

    lax.fori_loop(0, used, drain, 0)
    for step in range(N_X):
        put_meta(step).wait()


def pack_stage(a_tags, a_rows, a_count, a_tiles):
    return pl.pallas_call(
        pack_kernel,
        out_shape=(jax.ShapeDtypeStruct((WIDE, PAGE, TILE), jnp.bfloat16),) * N_X,
        in_specs=[pl.BlockSpec(memory_space=SMEM)] * 3 + [pl.BlockSpec(memory_space=VMEM)],
        out_specs=(pl.BlockSpec(memory_space=ANY),) * N_X,
        scratch_shapes=[
            pltpu.VMEM((N_DOC, META, TILE), jnp.bfloat16),
            pltpu.SMEM((N_DOC,), jnp.int32),
            pltpu.SMEM((N_DOC * 4,), jnp.int32),
            pltpu.SemaphoreType.DMA((a_tiles.shape[0],)),
            pltpu.SemaphoreType.DMA((N_X,)),
        ],
        name="pack",
    )(a_tags, a_rows, a_count, a_tiles)


def text_kernel(rows, cols, count, seed, offsets, tiles, out, acc, base):
    step = pl.program_id(0)

    @pl.when(step == 0)
    def _():
        row_iota = lax.broadcasted_iota(jnp.int32, (TILE, SKETCH), 0)
        col_iota = lax.broadcasted_iota(jnp.int32, (TILE, SKETCH), 1)
        start = (row_iota * SKETCH + col_iota) ^ (seed[0] * 747796405)
        base[...] = start ^ shr(start, 16)
        acc[...] = jnp.zeros_like(acc)

    doc = lax.axis_index("doc")
    first = offsets[doc] - offsets[doc - lax.rem(doc, 2)]
    slab = lax.axis_index("feat") * (TERMS // (TILE * N_FEAT))
    used = count[0]

    def some(width, first_at, group, carry):
        products = []
        for lane in range(width):
            at = first_at + group * width + lane
            block = (cols[step * CHUNK + at] + slab) * (TILE * SKETCH)
            block = block ^ lax.shift_right_logical(block, jnp.int32(16))
            mixing = base[...] ^ block
            mixing = mixing * 2146121005
            mixing = mixing ^ shr(mixing, 15)
            mixing = mixing * -2073254261
            mixing = mixing ^ shr(mixing, 16)
            levels = (shr(mixing, 8) & 65535).astype(jnp.float32)
            panel = ((levels - 32767.5) * (3.4641016 / 65536.0)).astype(jnp.bfloat16)
            products.append(jnp.dot(tiles[at], panel, preferred_element_type=jnp.float32))
        for lane in range(width):
            at = step * CHUNK + first_at + group * width + lane
            acc[rows[at] + first] += products[lane]
        return carry

    left = jnp.clip(used - step * CHUNK, 0, CHUNK)
    whole = left // GROUP
    lax.fori_loop(0, whole, functools.partial(some, GROUP, 0), 0)
    lax.fori_loop(0, left - whole * GROUP, functools.partial(some, 1, whole * GROUP), 0)

    @pl.when(step == pl.num_programs(0) - 1)
    def _():
        out[...] = acc[...].astype(jnp.bfloat16)


def text_stage(b_rows, b_cols, b_count, omega_seed, b_offsets, b_tiles):
    rows_shape = (PAIR_MAX, TILE, SKETCH)
    return pl.pallas_call(
        text_kernel,
        out_shape=jax.ShapeDtypeStruct(rows_shape, jnp.bfloat16),
        grid=(b_tiles.shape[0] // CHUNK,),
        in_specs=[pl.BlockSpec(memory_space=SMEM)] * 5
        + [pl.BlockSpec((CHUNK, TILE, TILE), lambda i: (i, 0, 0))],
        out_specs=pl.BlockSpec(rows_shape, lambda i: (0, 0, 0)),
        scratch_shapes=[
            pltpu.VMEM(rows_shape, jnp.float32),
            pltpu.VMEM((TILE, SKETCH), jnp.int32),
        ],
        cost_estimate=pl.CostEstimate(
            flops=20000000000, bytes_accessed=40000000, transcendentals=0
        ),
        name="text",
    )(b_rows, b_cols, b_count, omega_seed, b_offsets, b_tiles)


def sum_kernel(
    partial, tiles, rows, near, own, core_in, sums, feat_in, core_sem, load_sem, feat_sem, near_sem
):
    depth = rows.shape[0]
    doc = lax.axis_index("doc")
    feat = lax.axis_index("feat")
    core = lax.rem(doc, N_CORE)
    sibling = (doc - core + (1 - core), feat)

    def other(step):
        return lax.rem(feat + step, N_FEAT)

    lane = lax.rem(doc, WIDE)

    def beside(step):
        return lax.rem(lane + step, WIDE)

    barrier = pltpu.get_barrier_semaphore()

    def greet(step, carry):
        pl.semaphore_signal(
            barrier, inc=1, device_id=(doc - lane + beside(step), feat), device_id_type=MESH
        )
        return carry

    lax.fori_loop(1, WIDE, greet, 0)
    for step in range(1, N_FEAT):
        pl.semaphore_signal(barrier, inc=1, device_id=(doc, other(step)), device_id_type=MESH)
    pl.semaphore_wait(barrier, WIDE - 1 + N_FEAT - 1)

    from_core = pltpu.make_async_remote_copy(
        src_ref=partial.at[:, 1 - core],
        dst_ref=core_in,
        send_sem=core_sem.at[0],
        recv_sem=core_sem.at[1],
        device_id=sibling,
        device_id_type=MESH,
    )
    from_core.start()
    load = pltpu.make_async_copy(partial.at[:, core], own, load_sem)
    load.start()

    def tiles_to(step):
        return pltpu.make_async_remote_copy(
            src_ref=tiles.at[beside(step)],
            dst_ref=near.at[lane],
            send_sem=near_sem.at[0, step],
            recv_sem=near_sem.at[1, step],
            device_id=(doc - lane + beside(step), feat),
            device_id_type=MESH,
        )

    def send_tiles(step, carry):
        tiles_to(step).start()
        return carry

    lax.fori_loop(1, WIDE, send_tiles, 0)
    keep = pltpu.make_async_copy(tiles.at[lane], near.at[lane], near_sem.at[0, 0])
    keep.start()
    load.wait()
    from_core.wait()

    def to_feat(step):
        return pltpu.make_async_remote_copy(
            src_ref=sums.at[other(step)],
            dst_ref=feat_in.at[step - 1],
            send_sem=feat_sem.at[0, step],
            recv_sem=feat_sem.at[1, step],
            device_id=(doc, other(step)),
            device_id_type=MESH,
        )

    for step in (2, 1, 3, 0):
        to = other(step)
        for k in range(depth):
            sums[to, k] = own[k, to] + core_in[k, to]
        if step:
            to_feat(step).start()
    for step in (1, 3, 2):
        to_feat(step).wait_recv()
    for k in range(depth):
        terms = [
            block[k].astype(jnp.float32)
            for block in (sums.at[feat], feat_in.at[0], feat_in.at[1], feat_in.at[2])
        ]
        rows[k] = ((terms[0] + terms[1]) + (terms[2] + terms[3])).astype(jnp.bfloat16)
    for step in (1, 2, 3):
        to_feat(step).wait_send()

    def settle(step, carry):
        tiles_to(step).wait_recv()
        tiles_to(step).wait_send()
        return carry

    lax.fori_loop(1, WIDE, settle, 0)
    keep.wait()


def sum_stage(partial, tiles):
    bf16 = jnp.bfloat16
    dma = pltpu.SemaphoreType.DMA
    depth = PAIR_MAX // 8
    block = (TILE, SKETCH)
    return pl.pallas_call(
        sum_kernel,
        out_shape=(
            jax.ShapeDtypeStruct((depth,) + block, bf16),
            jax.ShapeDtypeStruct((WIDE, PAGE, TILE), bf16),
        ),
        in_specs=[pl.BlockSpec(memory_space=ANY)] * 2,
        out_specs=(pl.BlockSpec(memory_space=VMEM), pl.BlockSpec(memory_space=ANY)),
        scratch_shapes=[
            pltpu.VMEM((depth, N_FEAT) + block, bf16),
            pltpu.VMEM((depth, N_FEAT) + block, bf16),
            pltpu.VMEM((N_FEAT, depth) + block, bf16),
            pltpu.VMEM((N_FEAT - 1, depth) + block, bf16),
            dma((2,)),
            dma,
            dma((2, 4)),
            dma((2, WIDE)),
        ],
        compiler_params=pltpu.CompilerParams(collective_id=1, has_side_effects=True),
        cost_estimate=pl.CostEstimate(
            flops=20000000000, bytes_accessed=40000000, transcendentals=0
        ),
        name="sum",
    )(partial.reshape(depth, N_CORE, N_FEAT, TILE, SKETCH), tiles)


def exchange_kernel(
    depth,
    rows,
    tiles_1,
    tiles_2,
    tiles_3,
    main,
    side,
    inbox,
    place_sem,
    z_sem,
    second_sem,
    third_sem,
    pair_sem,
    tiles_sem,
    keep_sem,
):
    count = main.shape[4]
    main_own = rows.at[pl.ds(0, count)]
    side_own = rows.at[pl.ds(count, depth - count)]
    doc = lax.axis_index("doc")
    feat = lax.axis_index("feat")
    core = lax.rem(doc, N_CORE)
    z = lax.rem(doc // N_CORE, N_Z)
    x = doc // (N_CORE * N_Z)
    lane = z * N_CORE + core

    def device(x_to, z_to, core_to, feat_to):
        return ((x_to * N_Z + z_to) * N_CORE + core_to, feat_to)

    def turn(value, step, size):
        return lax.rem(value + (step % size), size)

    sibling = device(x, z, 1 - core, feat)

    def remote(source, target, sems, to):
        return pltpu.make_async_remote_copy(
            src_ref=source,
            dst_ref=target,
            send_sem=sems[0],
            recv_sem=sems[1],
            device_id=to,
            device_id_type=MESH,
        )

    barrier = pltpu.get_barrier_semaphore()

    def greet(step, carry):
        other = lax.rem(lane + step, N_Z * N_CORE)
        pl.semaphore_signal(
            barrier, inc=1, device_id=(x * (N_Z * N_CORE) + other, feat), device_id_type=MESH
        )
        return carry

    lax.fori_loop(1, N_Z * N_CORE, greet, 0)
    for step in (1, 3):
        pl.semaphore_signal(
            barrier, inc=1, device_id=device(turn(x, step, N_X), z, core, feat), device_id_type=MESH
        )
    for step in (1, 3):
        pl.semaphore_signal(
            barrier, inc=1, device_id=device(x, z, core, turn(feat, step, N_FEAT)), device_id_type=MESH
        )
    pl.semaphore_wait(barrier, N_Z * N_CORE - 1 + 4)

    place_main = pltpu.make_async_copy(main_own, main.at[core, feat, x, z], place_sem.at[0])
    place_side = pltpu.make_async_copy(side_own, side.at[core, x, feat, z], place_sem.at[1])
    place_main.start()
    place_side.start()

    upper = TILE // 2

    def ring_z(way, which, step):
        sign = 1 if way == 0 else -1
        block = turn(z, -sign * (step - 1), N_Z)
        held = main.at[core, feat, x, block] if which == 0 else side.at[core, x, feat, block]
        source = held if step > 1 else (main_own if which == 0 else side_own)
        if step == N_Z // 2:
            part = pl.ds(way * upper, upper)
            held = held.at[:, part]
            source = source.at[:, part]
        return remote(
            source, held, (z_sem.at[0, way, which, step], z_sem.at[1, way, which, step]),
            device(x, turn(z, sign, N_Z), core, feat),
        )

    def spread(block, mine):
        half = N_Z // 2
        for sems, at, axis, which in (
            (second_sem, 1, 1, 1),
            (second_sem, 0, 0, 0),
            (third_sem, 0, 1, 0),
            (third_sem, 4, 0, 1),
        ):
            held = (main.at[core, feat, x] if which == 0 else side.at[core, x, feat]).at[block]
            source = held
            if mine:
                source = main_own if which == 0 else side_own
            for way in range(2):
                sign = 1 if way == 0 else -1
                if axis == 0:
                    to = device(turn(x, sign, N_X), z, core, feat)
                else:
                    to = device(x, z, core, turn(feat, sign, N_FEAT))
                part = block // half
                number = way * 3 + (part if way == 0 else 1 - part)
                remote(source, held, (sems.at[0, at, number], sems.at[1, at, number]), to).start()

    for step in range(1, N_Z // 2 + 1):
        for way in range(2):
            for which in range(2):
                if step > 1:
                    ring_z(way, which, step - 1).wait_recv()
                ring_z(way, which, step).start()
        if step == 1:
            spread(z, True)
        else:
            spread(turn(z, 1 - step, N_Z), False)
            spread(turn(z, step - 1, N_Z), False)
    for way in range(2):
        for which in range(2):
            ring_z(way, which, N_Z // 2).wait_recv()
    spread(turn(z, N_Z // 2, N_Z), False)
    place_main.wait()
    place_side.wait()

    half = N_Z // 2

    def ring_four(sems, at, axis, block, kind):
        way, part, hop = kind
        sign = 1 if way == 0 else -1
        if axis == 0:
            place, to = x, device(turn(x, sign, N_X), z, core, feat)
        else:
            place, to = feat, device(x, z, core, turn(feat, sign, N_FEAT))
        ref = block(turn(place, -sign * (hop - 1), 4)).at[pl.ds(part * half, half)]
        number = way * 3 + (part ^ way if hop == 1 else 2)
        return remote(ref, ref, (sems.at[0, at, number], sems.at[1, at, number]), to)

    first_kinds = ((0, 0, 1), (1, 1, 1), (0, 1, 1), (1, 0, 1))
    later_kinds = ((0, 0, 2), (1, 1, 2))

    def main_block(feat_at, x_at):
        return main.at[core, feat_at, x_at]

    def side_block(x_at, feat_at):
        return side.at[core, x_at, feat_at]

    def second(which, kind):
        if which == 0:
            return ring_four(second_sem, 0, 0, lambda i: main_block(feat, i), kind)
        return ring_four(second_sem, 1, 1, lambda i: side_block(x, i), kind)

    def third(which, step, kind):
        if which == 0:
            chunk = turn(x, step, N_X)
            return ring_four(third_sem, step, 1, lambda i: main_block(i, chunk), kind)
        chunk = turn(feat, step, N_FEAT)
        return ring_four(third_sem, 4 + step, 0, lambda i: side_block(i, chunk), kind)

    def to_sibling(which, far, step):
        if which == 0:
            ref = main_block(turn(feat, far, N_FEAT), turn(x, step, N_X))
        else:
            ref = side_block(turn(x, far, N_X), turn(feat, step, N_FEAT))
        at = which * 16 + far * 4 + step
        return remote(ref, ref, (pair_sem.at[0, at], pair_sem.at[1, at]), sibling)

    to_sibling(0, 0, 0).start()
    to_sibling(1, 0, 0).start()

    def tiles_to(step, source, from_x):
        other = lax.rem(lane + step, N_Z * N_CORE)
        return remote(
            source.at[other], inbox.at[from_x, lane],
            (tiles_sem.at[0, from_x, step], tiles_sem.at[1, from_x, step]),
            (x * (N_Z * N_CORE) + other, feat),
        )

    def send_tiles(source, from_x, at):
        def one(step, carry):
            tiles_to(step, source, from_x).start()
            return carry

        lax.fori_loop(1, N_Z * N_CORE, one, 0)
        pltpu.make_async_copy(source.at[lane], inbox.at[from_x, lane], keep_sem.at[at]).start()

    for step, source in enumerate((tiles_1, tiles_2, tiles_3)):
        send_tiles(source, step, step)

    def pass_on_second(which):
        for kind in later_kinds:
            way, part, _ = kind
            second(which, (way, part, 1)).wait_recv()
            second(which, kind).start()

    def finish_second(which):
        second(which, (0, 1, 1)).wait_recv()
        for kind in first_kinds:
            third(which, 3, kind).start()
        to_sibling(which, 0, 3).start()
        second(which, (1, 0, 1)).wait_recv()
        for kind in first_kinds:
            third(which, 1, kind).start()
        to_sibling(which, 0, 1).start()

    def finish_far(which):
        for kind in later_kinds:
            second(which, kind).wait_recv()
        for kind in first_kinds:
            third(which, 2, kind).start()
        to_sibling(which, 0, 2).start()

    def pass_on_third(which, step):
        for kind in later_kinds:
            way, part, _ = kind
            third(which, step, (way, part, 1)).wait_recv()
            third(which, step, kind).start()

    def finish_third(which, step):
        third(which, step, (0, 1, 1)).wait_recv()
        to_sibling(which, 3, step).start()
        third(which, step, (1, 0, 1)).wait_recv()
        to_sibling(which, 1, step).start()
        for kind in later_kinds:
            third(which, step, kind).wait_recv()
        to_sibling(which, 2, step).start()

    pass_on_second(1)
    pass_on_second(0)
    finish_second(1)
    finish_second(0)
    pass_on_third(1, 0)
    pass_on_third(0, 0)
    finish_far(1)
    finish_far(0)
    finish_third(1, 0)
    finish_third(0, 0)
    for step in (3, 1, 2):
        pass_on_third(1, step)
        pass_on_third(0, step)
        finish_third(1, step)
        finish_third(0, step)

    for which in range(2):
        for far in range(4):
            for step in range(4):
                to_sibling(which, far, step).wait_recv()
                to_sibling(which, far, step).wait_send()
        for kind in first_kinds + later_kinds:
            second(which, kind).wait_send()
        for step in range(4):
            for kind in first_kinds + later_kinds:
                third(which, step, kind).wait_send()
        for way in range(2):
            for step in range(1, N_Z // 2 + 1):
                ring_z(way, which, step).wait_send()
    def settle(from_x, carry):
        def one(step, inner):
            copy = tiles_to(step, tiles_1, from_x)
            copy.wait_recv()
            copy.wait_send()
            return inner

        lax.fori_loop(1, N_Z * N_CORE, one, 0)
        pltpu.make_async_copy(tiles_1.at[0], inbox.at[0, 0], keep_sem.at[from_x]).wait()
        return carry

    lax.fori_loop(0, N_X - 1, settle, 0)


def exchange_stage(depth, rows, tiles):
    bf16 = jnp.bfloat16
    dma = pltpu.SemaphoreType.DMA
    block = (TILE, SKETCH)
    first = (depth + 1) // 2
    main, side, inbox = pl.pallas_call(
        functools.partial(exchange_kernel, depth),
        out_shape=(
            jax.ShapeDtypeStruct((N_CORE, N_FEAT, N_X, N_Z, first) + block, bf16),
            jax.ShapeDtypeStruct((N_CORE, N_X, N_FEAT, N_Z, depth - first) + block, bf16),
            jax.ShapeDtypeStruct((N_X - 1, WIDE, PAGE, TILE), bf16),
        ),
        in_specs=[pl.BlockSpec(memory_space=VMEM)] + [pl.BlockSpec(memory_space=ANY)] * (N_X - 1),
        out_specs=(pl.BlockSpec(memory_space=ANY),) * 3,
        scratch_shapes=[
            dma((2,)),
            dma((2, 2, 2, N_Z // 2 + 1)),
            dma((2, 2, 6)),
            dma((2, 8, 6)),
            dma((2, 32)),
            dma((2, N_X - 1, WIDE)),
            dma((N_X - 1,)),
        ],
        compiler_params=pltpu.CompilerParams(collective_id=depth, has_side_effects=True),
        name="exchange_%d" % depth,
    )(rows, *tiles)
    return (
        main.reshape((-1,) + block),
        side.reshape((-1,) + block),
        inbox.reshape(N_DOC - WIDE, PAGE, TILE),
    )


def final_kernel(
    depth, notes, b_offsets, a_offsets, near, far, main, side,
    out, inbox, lists, zbuf, sems, tile_sems,
):
    first_count = (depth + 1) // 2
    loads = (
        pltpu.make_async_copy(near, inbox.at[pl.ds(0, WIDE)], tile_sems.at[0]),
        pltpu.make_async_copy(far, inbox.at[pl.ds(WIDE, N_DOC - WIDE)], tile_sems.at[1]),
    )
    for load in loads:
        load.start()
    here = lax.axis_index("doc") // WIDE

    def fetch(ref, at, slot):
        group = lax.shift_right_logical(slot, jnp.int32(2))
        return pltpu.make_async_copy(ref.at[at], zbuf.at[slot], sems.at[group])

    def listed(number, found):
        way = lax.shift_right_logical(number, jnp.int32(4))
        step = way + jnp.where(way == 2, 1, 0) - jnp.where(way == 3, 1, 0)
        doc = ((here - step) & (N_X - 1)) * WIDE + (number & (WIDE - 1))
        shift = a_offsets[doc]
        split = b_offsets[doc]
        before = jnp.maximum(doc - 1, 0)
        chips = [lax.shift_right_logical(at, jnp.int32(1)) for at in (before, doc)]
        bases = [shift - b_offsets[chip * 2] for chip in chips]
        for rank in range(2):
            tag = notes[number * 4 + rank * 2] - 1

            @pl.when(tag >= 0)
            def _():
                row = notes[number * 4 + rank * 2 + 1]
                early = row + shift < split
                chip = jnp.where(early, chips[0], chips[1])
                inner = jnp.clip(row + jnp.where(early, bases[0], bases[1]), 0, depth * 8 - 1)
                k = lax.shift_right_logical(inner, jnp.int32(3))
                core = lax.shift_right_logical(inner, jnp.int32(2)) & 1
                feat = inner & 3
                x = lax.shift_right_logical(chip, jnp.int32(3))
                z = chip & 7
                lists[0, found] = tag
                lists[1, found] = number * 2 + rank

                @pl.when(k < first_count)
                def _():
                    at = (((core * N_FEAT + feat) * N_X + x) * N_Z + z) * first_count + k
                    fetch(main, at, found).start()

                @pl.when(k >= first_count)
                def _():
                    at = (((core * N_X + x) * N_FEAT + feat) * N_Z + z) * (
                        depth - first_count
                    ) + (k - first_count)
                    fetch(side, at, found).start()

            found = found + (tag >= 0).astype(jnp.int32)
        return found

    total = lax.fori_loop(0, N_DOC, listed, 0)
    groups = (total + TOGETHER - 1) // TOGETHER

    def fill(at, carry):
        lists[0, at] = 0
        lists[1, at] = 0
        fetch(main, 0, at).start()
        return carry

    lax.fori_loop(total, groups * TOGETHER, fill, 0)
    out[...] = jnp.zeros_like(out)
    for load in loads:
        load.wait()

    def add(group, carry):
        first = group * TOGETHER
        pltpu.make_async_copy(
            main.at[pl.ds(0, TOGETHER)], zbuf.at[pl.ds(first, TOGETHER)], sems.at[group]
        ).wait()
        products = []
        for lane in range(TOGETHER):
            at = first + lane
            source = lists[1, at]
            start = pl.multiple_of((source & 1) * TILE, TILE)
            tile = inbox[lax.shift_right_logical(source, jnp.int32(1)), pl.ds(start, TILE), :]
            product = lax.dot_general(
                tile, zbuf[at], (((0,), (0,)), ((), ())), preferred_element_type=jnp.float32
            )
            products.append(jnp.where(at < total, product, 0.0))
        for lane in range(TOGETHER):
            place = pl.multiple_of(lists[0, first + lane] * TILE, TILE)
            out[pl.ds(place, TILE), :] += products[lane]
        return carry

    lax.fori_loop(0, groups, add, 0)


def final_stage(depth, notes, b_offsets, a_offsets, near, far, main, side):
    return pl.pallas_call(
        functools.partial(final_kernel, depth),
        out_shape=jax.ShapeDtypeStruct((TAG_DEV, SKETCH), jnp.float32),
        in_specs=[
            pl.BlockSpec(memory_space=SMEM),
            pl.BlockSpec(memory_space=SMEM),
            pl.BlockSpec(memory_space=SMEM),
            pl.BlockSpec(memory_space=ANY),
            pl.BlockSpec(memory_space=ANY),
            pl.BlockSpec(memory_space=ANY),
            pl.BlockSpec(memory_space=ANY),
        ],
        out_specs=pl.BlockSpec(memory_space=VMEM),
        scratch_shapes=[
            pltpu.VMEM((N_DOC, PAGE, TILE), jnp.bfloat16),
            pltpu.SMEM((2, DEPTH), jnp.int32),
            pltpu.VMEM((DEPTH, TILE, SKETCH), jnp.bfloat16),
            pltpu.SemaphoreType.DMA((DEPTH // TOGETHER,)),
            pltpu.SemaphoreType.DMA((2,)),
        ],
    )(notes, b_offsets, a_offsets, near, far, main, side)


def local(
    b_tiles,
    b_rows,
    b_cols,
    b_count,
    b_offsets,
    a_tiles,
    a_rows,
    a_tags,
    a_count,
    a_offsets,
    omega_seed,
):
    tiles = pack_stage(a_tags[:, 0], a_rows[:, 0], a_count[:, 0], a_tiles)
    moved = []
    for step in (1, 3, 2):
        route = [(at, (at + step * WIDE) % N_DOC) for at in range(N_DOC)]
        moved.append(lax.ppermute(tiles[step], "doc", route))
    partial = text_stage(
        b_rows[:, 0], b_cols[:, 0], b_count[:, 0], omega_seed, b_offsets, b_tiles
    )
    mine, near = sum_stage(partial, tiles[0])

    def rest(depth, rows, near, *tiles):
        main, side, far = exchange_stage(depth, rows, tiles)
        notes = jnp.concatenate([near[:, 2 * TILE, 0:4], far[:, 2 * TILE, 0:4]])
        notes = notes.astype(jnp.int32).reshape(-1)
        return final_stage(depth, notes, b_offsets, a_offsets, near, far, main, side)

    most = jnp.max(b_offsets[2::2] - b_offsets[:-1:2])
    return lax.cond(
        most <= 16, functools.partial(rest, 2), functools.partial(rest, 3), mine, near, *moved
    )


def solution(mesh):
    return jax.shard_map(
        local,
        mesh=mesh,
        in_specs=(
            P("doc", "feat", None),
            P("doc", "feat"),
            P("doc", "feat"),
            P("doc", "feat"),
            P(),
            P("doc", "feat", None),
            P("doc", "feat"),
            P("doc", "feat"),
            P("doc", "feat"),
            P(),
            P(),
        ),
        out_specs=P(("doc", "feat"), None),
        check_vma=False,
    )
```
